32 devices in a mesh: sec: 8 (over y, x, core), mpo: 4 (over z).
Axes of the slice: x: 2, y: 2, z: 4, core: 2. Of those that a mesh axis runs over, the one named last changes fastest.
Arguments:
- guess: float32 [6144, 256], P('sec'), may hold values from -6 to 6
- left_env: bfloat16 [20, 6144, 768], P('mpo', 'sec'), may hold values from -0.21875 to 0.21875
- right_env: bfloat16 [20, 2048, 256], P('mpo', 'sec'), may hold values from -0.375 to 0.375
- block_rows: int32 [8], replicated, may hold values from 1 to 768, 2048 in all
- charges: int32 [20], P('mpo'), may hold values from -2 to 2, as said below
- ranks: int32 [8], replicated, may hold values from 1 to 256
Outputs:
- wavefunction: float32 [6144, 256], P(('sec', 'mpo'))
- truncated: float32 [6144, 256], P(('sec', 'mpo'))
The draws below stay inside these ranges and needn't reach their ends.
Inputs may be any that keep to these rules, and one draw needn't show every extreme that they name: The 5 terms of one index of mpo (each aligned run of 5 terms) carry the charges -2, -1, 0, 1, 2 once each.
All inputs are finite; a program needn't handle non-finite values.
Results may differ from the reference program's by a relative error of at most 0.01.
Values may be sent and summed in bfloat16 or wider, within the bound.
A program may use at most 64 MiB of HBM per device.

```python
import math
import jax
import jax.numpy as jnp
import numpy as np
from jax import lax

MEAN = 256
RB = 256
ITERS = 4
CAP = 768
NSEC = 8
TERMS = 20


def draw_charges(key, part):
    subkeys = jax.random.split(jax.random.fold_in(key, 7), TERMS // 5)
    groups = jax.vmap(lambda subkey: jax.random.permutation(subkey, 5))(subkeys)
    return (groups.reshape(-1) - 2).astype(jnp.int32)


def place_ends(array, key, least, largest):
    place = [jax.random.randint(jax.random.fold_in(key, axis), (), 0, length) for axis, length in enumerate(array.shape)]
    main_axis = array.shape.index(max(array.shape))
    beside = place[:main_axis] + [(place[main_axis] + 1) % array.shape[main_axis]] + place[main_axis + 1:]
    return array.at[tuple(place)].set(least).at[tuple(beside)].set(largest)


def block_levels(rng, dims, pieces, smallest, largest):
    def one(position, shards_of):
        steps = jax.random.uniform(jax.random.fold_in(jax.random.fold_in(rng, 6), position), (shards_of,), jnp.float32, smallest / len(pieces), largest / len(pieces))
        return jnp.repeat(jnp.exp(steps), dims[position] // shards_of).reshape((-1,) + (1,) * (len(dims) - position - 1))

    gain = one(*pieces[0])
    for cut in pieces[1:]:
        gain = gain * one(*cut)
    return gain


def length_profile(amount, total, most, skew):
    loads = [(1 << 20) // math.isqrt(rank ** skew) + 1 for rank in range(2, amount + 1)]
    rest, given = total - most - (amount - 1), [1] * (amount - 1)
    while rest > 0:
        free = [i for i in range(amount - 1) if given[i] < most]
        whole, remaining = sum([loads[i] for i in free]), rest
        for i in free:
            addition = min(most - given[i], max(1, remaining * loads[i] // whole), rest)
            given[i] = given[i] + addition
            rest = rest - addition
    return np.array([most] + given)


def ragged(stream_key, amount, total, most, lean):
    if amount == 2:
        one = jax.random.randint(stream_key, (), max(1, total - most), min(most, total - 1) + 1)
        return jnp.stack([one, total - one])
    tallies = jnp.asarray(length_profile(amount, total, most, lean), jnp.int32)
    twos = (amount - 1) // 2
    giver, taker = tallies[1:1 + 2 * twos:2], tallies[2:2 + 2 * twos:2]
    room = jnp.minimum(giver - 1, most - taker)
    moved = jax.random.randint(jax.random.fold_in(stream_key, 1), (twos,), 0, 1 << 20) % (room + 1)
    tallies = tallies.at[1:1 + 2 * twos:2].set(giver - moved).at[2:2 + 2 * twos:2].set(taker + moved)
    return tallies[jax.random.permutation(jax.random.fold_in(stream_key, 2), amount)]


def normal_values(stream_key, extent, spread, most, cuts=(), held_as=jnp.bfloat16):
    loudness = block_levels(stream_key, extent, cuts, -0.22, 0.18) if cuts else 1.0
    drawn = jax.random.normal(stream_key, extent, jnp.float32) * spread * loudness
    return jnp.minimum(jnp.maximum(drawn, -most), most).astype(held_as)


def setup_inputs(seed: int = 0) -> dict:
    key_of = jax.random.split(jax.random.key(seed), 7)
    return {
        "guess": normal_values(key_of[0], (NSEC * CAP, RB), 1.0, 6.0, ((0, 8),), jnp.float32),
        "left_env": normal_values(key_of[1], (TERMS, NSEC * CAP, CAP), CAP ** -0.5, 0.21875, ((0, 4), (1, 8))),
        "right_env": normal_values(key_of[2], (TERMS, NSEC * RB, RB), RB ** -0.5, 0.375, ((0, 4), (1, 8))),
        "block_rows": ragged(key_of[3], NSEC, MEAN * NSEC, CAP, 2).astype(jnp.int32),
        "charges": draw_charges(jax.random.fold_in(key_of[6], 71), 0),
        "ranks": place_ends(jax.random.randint(key_of[5], (NSEC,), 1, RB + 1), jax.random.fold_in(key_of[5], 1), 1, RB).astype(jnp.int32),
    }


epsilon = 1e-06
step_size = 0.1
highest = lax.Precision.HIGHEST

def apply_operator(current, left_blocks, right_blocks, charges, row_mask):
    rounded = current.astype(jnp.bfloat16)

    def add_term(running, inputs):
        left_term, right_term, charge = inputs
        shifted = jnp.roll(rounded, charge, axis=0)
        middle = jnp.einsum('sij,sjk->sik', left_term.astype(jnp.float32), shifted.astype(jnp.float32)).astype(jnp.bfloat16)
        summand = jnp.einsum('sik,skl->sil', middle.astype(jnp.float32), right_term.astype(jnp.float32))
        return (running + summand, None)
    applied, unused = lax.scan(add_term, jnp.zeros(current.shape, jnp.float32), (left_blocks, right_blocks, charges))
    return applied * row_mask

def solve_block(lower_factor, right_side):
    return jax.scipy.linalg.cho_solve((lower_factor, True), right_side.T).T

def reference(guess, left_env, right_env, block_rows, charges, ranks):
    entries = MEAN * NSEC * RB
    positions = jnp.arange(CAP, dtype=jnp.int32)
    row_mask = (positions[None, :] < block_rows[:, None]).astype(jnp.float32)[:, :, None]
    current = guess.reshape(NSEC, CAP, RB) * row_mask
    current = current * lax.rsqrt(jnp.sum(current * current) / entries + epsilon)
    left_blocks = left_env.reshape(TERMS, NSEC, CAP, CAP)
    right_blocks = right_env.reshape(TERMS, NSEC, RB, RB)
    for repeat in range(ITERS):
        applied = apply_operator(current, left_blocks, right_blocks, charges.astype(jnp.int32), row_mask)
        rayleigh = jnp.sum(current * applied) / (jnp.sum(current * current) + epsilon)
        update = current - step_size * (applied - rayleigh * current)
        current = update * lax.rsqrt(jnp.sum(update * update) / entries + epsilon)
    density = jnp.einsum('sij,sik->sjk', current, current, precision=highest)
    columns = (jnp.arange(RB, dtype=jnp.int32)[None, :] < ranks[:, None]).astype(jnp.float32)
    span_basis = (jnp.eye(RB, dtype=jnp.float32)[None] + density / MEAN) * columns[:, None, :]
    gram_matrix = jnp.einsum('sij,sik->sjk', span_basis, span_basis, precision=highest) + jax.vmap(jnp.diag)(1.0 - columns)
    factor = jnp.linalg.cholesky(gram_matrix)
    coords = jnp.einsum('sij,sjk->sik', current, span_basis, precision=highest)
    solved = jax.vmap(solve_block)(factor, coords)
    truncated = jnp.einsum('sik,sjk->sij', solved, span_basis, precision=highest)
    return (current.reshape(NSEC * CAP, RB), truncated.reshape(NSEC * CAP, RB))
```

```python
import functools

import jax
import jax.numpy as jnp
from jax import lax
from jax.experimental import pallas as pl
from jax.experimental.pallas import tpu as pltpu
from jax.sharding import PartitionSpec as P

MEAN = 256
ITERS = 4


epsilon = 1e-06
step_size = 0.1
highest = lax.Precision.HIGHEST


PIECES = 2


def row_sum(values):
    return jnp.sum(jnp.sum(values.reshape(-1, 8, 128), axis=0), axis=0, keepdims=True)


def arrival_order(member, members):
    steps = [(-1, 1), (1, -1)][member >= members // 2]
    order = [member]
    for d in range(1, members):
        order += [member + s * d for s in steps if 0 <= member + s * d < members]
    return order


def reduce_order(member, members):
    order = arrival_order(member, members)[1:]
    far = 1 if member < members // 2 else -1
    return sorted(order, key=lambda other: -(abs(other - member) * 2 + ((other - member) * far > 0)))


def tile_order(member, members, tiles):
    return list(range(tiles)) if member < members // 2 else list(range(tiles))[::-1]


def tile_ready(members, tiles):
    ready = [0] * tiles
    for member in range(members):
        order = arrival_order(member, members)
        for i, tile in enumerate(tile_order(member, members, tiles)):
            chunks = range(tile * members // tiles, -(-(tile + 1) * members // tiles))
            ready[i] = max([ready[i]] + [order.index(c) for c in chunks])
    return ready


def iterate_kernel(
    sectors, members, entries,
    block_rows, charges, guess, left_hbm, right_hbm, slab, density,
    left, right, xbuf, acc, app_chunk, cur, rs_out, rs_in, scal,
    load_sem, z_s, z_r, n_s, n_r, f_s, f_r, b_s, b_r, p_s, p_r, rs_s, rs_r, sc_s, sc_r,
):
    sector = lax.axis_index("sec")
    member = lax.axis_index("mpo")
    capacity, width = guess.shape
    chunk = capacity // members
    piece = chunk // PIECES
    tiles = left.shape[1]
    terms = left.shape[0]
    chips = sectors // 2
    parity = lax.rem(sector, 2)
    chip = sector // 2
    odd = lax.rem(chip, 2)
    sibling = sector + 1 - 2 * parity
    ahead = lax.rem(sector + 2, sectors)
    behind = lax.rem(sector + sectors - 2, sectors)
    relayed = chips == 4
    interior = jnp.logical_and(member > 0, member < members - 1)
    has_up = member < members - 1
    has_down = member > 0
    always = None
    sends = []

    loads = [pltpu.make_async_copy(right_hbm, right, load_sem.at[tiles])]
    for i in range(tiles):
        loads.append(pltpu.make_async_copy(
            left_hbm.at[:, :, pl.ds(i * width, width)], left.at[:, i], load_sem.at[i]
        ))
    for load in loads:
        load.start()

    barrier = pltpu.get_barrier_semaphore()
    for d in range(1, sectors):
        pl.semaphore_signal(
            barrier, inc=1, device_id=(lax.rem(sector + d, sectors), member),
            device_id_type=pl.DeviceIdType.MESH,
        )
    for d in range(1, members):
        pl.semaphore_signal(
            barrier, inc=1, device_id=(sector, lax.rem(member + d, members)),
            device_id_type=pl.DeviceIdType.MESH,
        )
    pl.semaphore_wait(barrier, sectors + members - 2)

    def remote(src, dst, send, recv, sec, mpo):
        return pltpu.make_async_remote_copy(
            src_ref=src, dst_ref=dst, send_sem=send, recv_sem=recv,
            device_id=(sec, mpo), device_id_type=pl.DeviceIdType.MESH,
        )

    def launch(copy, when=always):
        if when is None:
            copy.start()
        else:
            pl.when(when)(copy.start)
        sends.append((copy, when))

    def by_member(table):
        value = jnp.int32(table[0])
        for m in range(1, members):
            value = jnp.where(member == m, table[m], value)
        return value

    def rows_of(j):
        return pl.ds(pl.multiple_of(j * chunk, chunk), chunk)

    def piece_of(j, q):
        return pl.ds(pl.multiple_of(j * chunk + q * piece, piece), piece)

    order = [by_member([arrival_order(m, members)[r] for m in range(members)]) for r in range(members)]
    targets = [by_member([reduce_order(m, members)[r] for m in range(members)]) for r in range(members - 1)]
    tile_at = [by_member([tile_order(m, members, tiles)[i] for m in range(members)]) for i in range(tiles)]
    ready = tile_ready(members, tiles)

    if relayed:
        near = jnp.where(odd == 1, behind, ahead)
        across = lax.rem(sector + sectors // 2, sectors)
        near_shift = jnp.where(odd == 1, 2, -2)
        pass_near = parity == odd
    else:
        near_shift = jnp.int32(-2)
        pass_near = parity == 0
    far_shift = -near_shift

    def z_send(k, j, q, up, when):
        rows = piece_of(j, q)
        step = 1 if up else -1
        launch(remote(
            xbuf.at[k, 0, rows], xbuf.at[k, 0, rows], z_s.at[k, int(up), j, q], z_r.at[k, j, q],
            sector, jnp.clip(member + step, 0, members - 1),
        ), when)

    def z_forward(k, j, q):
        z_send(k, j, q, True, jnp.logical_and(interior, j < member))
        z_send(k, j, q, False, jnp.logical_and(interior, j > member))

    def near_send(k, j, q):
        rows = piece_of(j, q)
        if relayed:
            launch(remote(
                xbuf.at[k, 0, rows], xbuf.at[k, 2, rows], n_s.at[k, j, q], n_r.at[k, j, q], near, member,
            ))
        else:
            launch(remote(
                xbuf.at[k, 0, rows], xbuf.at[k, 2, rows], n_s.at[k, j, q], n_r.at[k, j, q], behind, member,
            ))
            launch(remote(
                xbuf.at[k, 0, rows], xbuf.at[k, 3, rows], f_s.at[k, j, q], f_r.at[k, j, q], ahead, member,
            ))

    def far_send(k, j, q):
        rows = piece_of(j, q)
        if relayed:
            launch(remote(
                xbuf.at[k, 2, rows], xbuf.at[k, 3, rows], f_s.at[k, j, q], f_r.at[k, j, q], across, member,
            ))

    def sibling_send(k, j):
        rows = rows_of(j)
        launch(remote(
            xbuf.at[k, 0, rows], xbuf.at[k, 1, rows], b_s.at[k, j], b_r.at[k, j], sibling, member,
        ))

    def pass_send(k, j, slot, when):
        rows = rows_of(j)
        launch(remote(
            xbuf.at[k, slot, rows], xbuf.at[k, 4, rows], p_s.at[k, j], p_r.at[k, j], sibling, member,
        ), when)

    def arrived(k, slot, rows, send, recv):
        remote(xbuf.at[k, slot, rows], xbuf.at[k, slot, rows], send, recv, sibling, member).wait_recv()

    def rs_copy(k, r, q):
        return remote(
            rs_out.at[k, r, pl.ds(q * piece, piece)], rs_in.at[k, member, pl.ds(q * piece, piece)],
            rs_s.at[k, r, q], rs_r.at[k, member, q], sector, targets[r],
        )

    def scal_copy(k, d):
        return remote(
            scal.at[k, sector], scal.at[k, sector],
            sc_s.at[k, d - 1], sc_r.at[k, d - 1], lax.rem(sector + d, sectors), member,
        )

    def scal_wait(k):
        for d in range(1, sectors):
            src = lax.rem(sector - d + sectors, sectors)
            remote(
                scal.at[k, src], scal.at[k, src],
                sc_s.at[k, d - 1], sc_r.at[k, d - 1], src, member,
            ).wait_recv()

    def term_of(charge):
        index = jnp.int32(0)
        for i in range(1, terms):
            index = jnp.where(charges[i] == charge, i, index)
        return index

    slot_term = [
        term_of(0), term_of(2 * parity - 1), term_of(near_shift), term_of(far_shift),
        term_of(1 - 2 * parity),
    ]

    def add_tile(k, slot, i, first=False):
        index, tile = slot_term[slot], tile_at[i]
        rows = pl.ds(pl.multiple_of(tile * width, width), width)
        mixed = jnp.dot(
            xbuf[k, slot, rows, :], right[index], preferred_element_type=jnp.float32
        ).astype(jnp.bfloat16)
        value = jnp.dot(left[index, tile], mixed, preferred_element_type=jnp.float32)
        acc[...] = value if first else acc[...] + value

    def send_sums(k, first, second, third):
        rows = [row_sum(first), row_sum(second), row_sum(third), jnp.zeros((5, 128), jnp.float32)]
        scal[k, sector] = jnp.concatenate(rows, axis=0)
        for d in range(1, sectors):
            launch(scal_copy(k, d))

    def coefficients(k):
        sums = jnp.sum(jnp.sum(scal[k], axis=0), axis=1, keepdims=True)
        self_dot, cross_dot, image_dot = sums[0:1], sums[1:2], sums[2:3]
        if k == 0:
            scale = lax.rsqrt(self_dot / entries + epsilon)
            return scale, scale
        rayleigh = cross_dot / (self_dot + epsilon)
        squares = self_dot * (1.0 - (step_size * rayleigh) ** 2) + step_size**2 * image_dot
        scale = lax.rsqrt(squares / entries + epsilon)
        return (1.0 + step_size * rayleigh) * scale, -step_size * scale

    def state_sums(k, keep, add):
        if k == 0:
            send_sums(0, cur[...] * cur[...], jnp.zeros((8, 128)), jnp.zeros((8, 128)))
            return
        if k == 1:
            state = keep * cur[...]
        else:
            state = keep * cur[...] + add * xbuf[k - 1, 0].astype(jnp.float32)
        cur[...] = state
        applied = xbuf[k, 0].astype(jnp.float32)
        send_sums(k, state * state, state * applied, applied * applied)

    own_rows = block_rows[sector]
    positions = lax.broadcasted_iota(jnp.int32, (capacity, width), 0)
    start = jnp.where(positions < own_rows, guess[...], 0.0)
    xbuf[0, 0] = start.astype(jnp.bfloat16)
    cur[...] = start
    keep = add = None

    for k in range(ITERS):
        for r in range(members + 3):
            for q in range(PIECES):
                if r < members:
                    j = order[r]
                    if r > 0 and k > 0:
                        arrived(k, 0, piece_of(j, q), z_s.at[k, 0, j, q], z_r.at[k, j, q])
                        z_forward(k, j, q)
                    if r > 0 or k == 0:
                        near_send(k, j, q)
                if 1 <= r <= members:
                    j = order[r - 1]
                    arrived(k, 2, piece_of(j, q), n_s.at[k, j, q], n_r.at[k, j, q])
                    far_send(k, j, q)
                if 2 <= r <= members + 1:
                    j = order[r - 2]
                    arrived(k, 3, piece_of(j, q), f_s.at[k, j, q], f_r.at[k, j, q])
            if r < members:
                sibling_send(k, order[r])
            if 1 <= r <= members:
                pass_send(k, order[r - 1], 2, pass_near)
            if 2 <= r <= members + 1:
                pass_send(k, order[r - 2], 3, jnp.logical_not(pass_near))
            if r == 0 and k == 0:
                state_sums(0, None, None)
                for load in loads:
                    load.wait()
            for i in range(tiles):
                if ready[i] == r:
                    add_tile(k, 0, i, first=i == 0)
            if 1 <= r <= members:
                j = order[r - 1]
                arrived(k, 1, rows_of(j), b_s.at[k, j], b_r.at[k, j])
            if 3 <= r:
                j = order[r - 3]
                arrived(k, 4, rows_of(j), p_s.at[k, j], p_r.at[k, j])
            for slot, lag in ((1, 1), (2, 1), (3, 2), (4, 3)):
                for i in range(tiles):
                    if ready[i] == r - lag:
                        add_tile(k, slot, i)
            if r == members and k > 0:
                state_sums(k, keep, add)
        for q in range(PIECES):
            for t in range(members - 1):
                rs_out[k, t, pl.ds(q * piece, piece)] = acc[piece_of(targets[t], q), :].astype(jnp.bfloat16)
                launch(rs_copy(k, t, q))
        scal_wait(k)
        keep, add = coefficients(k)
        for q in range(PIECES):
            part = pl.ds(q * piece, piece)
            mine = piece_of(member, q)
            image = acc[mine, :]
            for r in range(1, members):
                j = order[r]
                remote(
                    rs_in.at[k, j, part], rs_in.at[k, j, part],
                    rs_s.at[k, 0, q], rs_r.at[k, j, q], sibling, member,
                ).wait_recv()
                image = image + rs_in[k, j, part].astype(jnp.float32)
            positions = lax.broadcasted_iota(jnp.int32, (piece, width), 0) + member * chunk + q * piece
            image = jnp.where(positions < own_rows, image, 0.0) * add
            if k > 0:
                image = image + keep * app_chunk[part, :]
            app_chunk[part, :] = image
            xbuf[k + 1, 0, mine] = image.astype(jnp.bfloat16)
            z_send(k + 1, member, q, True, has_up)
            z_send(k + 1, member, q, False, has_down)
            if k < ITERS - 1:
                near_send(k + 1, member, q)

    for r in range(1, members):
        for q in range(PIECES):
            j = order[r]
            arrived(ITERS, 0, piece_of(j, q), z_s.at[ITERS, 0, j, q], z_r.at[ITERS, j, q])
            z_forward(ITERS, j, q)
    state_sums(ITERS, keep, add)
    scal_wait(ITERS)
    keep, add = coefficients(ITERS)
    final = keep * cur[...] + add * xbuf[ITERS, 0].astype(jnp.float32)
    cur[...] = final
    slab[...] = cur[rows_of(member), :]
    density[...] = exact_dot(final, final, ((0,), (0,)))
    for copy, when in sends:
        if when is None:
            copy.wait_send()
        else:
            pl.when(when)(copy.wait_send)


def iterate(guess, left_env, right_env, block_rows, charges):
    capacity, width = guess.shape
    terms = left_env.shape[0]
    sectors = lax.axis_size("sec")
    members = lax.axis_size("mpo")
    chunk = capacity // members
    tiles = capacity // width
    entries = MEAN * sectors * width
    dma = pltpu.SemaphoreType.DMA
    vmem = pl.BlockSpec(memory_space=pltpu.VMEM)
    smem = pl.BlockSpec(memory_space=pltpu.SMEM)
    hbm = pl.BlockSpec(memory_space=pl.ANY)
    return pl.pallas_call(
        functools.partial(iterate_kernel, sectors, members, entries),
        out_shape=(
            jax.ShapeDtypeStruct((chunk, width), jnp.float32),
            jax.ShapeDtypeStruct((width, width), jnp.float32),
        ),
        in_specs=[smem, smem, vmem, hbm, hbm],
        out_specs=(vmem, vmem),
        scratch_shapes=[
            pltpu.VMEM((terms, tiles, capacity, width), left_env.dtype),
            pltpu.VMEM((terms, width, width), right_env.dtype),
            pltpu.VMEM((ITERS + 1, 5, capacity, width), jnp.bfloat16),
            pltpu.VMEM((capacity, width), jnp.float32),
            pltpu.VMEM((chunk, width), jnp.float32),
            pltpu.VMEM((capacity, width), jnp.float32),
            pltpu.VMEM((ITERS, members - 1, chunk, width), jnp.bfloat16),
            pltpu.VMEM((ITERS, members, chunk, width), jnp.bfloat16),
            pltpu.VMEM((ITERS + 1, sectors, 8, 128), jnp.float32),
            dma((tiles + 1,)),
            dma((ITERS + 1, 2, members, PIECES)),
            dma((ITERS + 1, members, PIECES)),
            dma((ITERS, members, PIECES)),
            dma((ITERS, members, PIECES)),
            dma((ITERS, members, PIECES)),
            dma((ITERS, members, PIECES)),
            dma((ITERS, members)),
            dma((ITERS, members)),
            dma((ITERS, members)),
            dma((ITERS, members)),
            dma((ITERS, members - 1, PIECES)),
            dma((ITERS, members, PIECES)),
            dma((ITERS + 1, sectors)),
            dma((ITERS + 1, sectors)),
        ],
        compiler_params=pltpu.CompilerParams(
            collective_id=0, has_side_effects=True, vmem_limit_bytes=56 * 1024 * 1024
        ),
    )(block_rows, charges, guess, left_env, right_env)


BLOCK = 64


def exact_dot(left, right, dims):
    return lax.dot_general(
        left, right, (dims, ((), ())), precision=highest, preferred_element_type=jnp.float32
    )


def inverse_factor(block):
    rows = lax.broadcasted_iota(jnp.int32, (BLOCK, BLOCK), 0)
    lanes = lax.broadcasted_iota(jnp.int32, (BLOCK, BLOCK), 1)
    joined = jnp.concatenate([block, jnp.where(rows == lanes, 1.0, 0.0)], axis=1)
    tiles = [joined[8 * i:8 * i + 8, :] for i in range(BLOCK // 8)]
    below = lax.broadcasted_iota(jnp.int32, (8, 1), 0)
    for j in range(BLOCK):
        home, offset = divmod(j, 8)
        row = tiles[home][offset:offset + 1, :]
        scaled = row / row[:, j:j + 1]
        for i in range(home, BLOCK // 8):
            column = tiles[i][:, j:j + 1]
            if i == home:
                if offset == 7:
                    continue
                column = jnp.where(below > offset, column, 0.0)
            tiles[i] = tiles[i] - column * scaled
    joined = jnp.concatenate(tiles, axis=0)
    wide_rows = lax.broadcasted_iota(jnp.int32, joined.shape, 0)
    wide_lanes = lax.broadcasted_iota(jnp.int32, joined.shape, 1)
    pivots = jnp.sum(jnp.where(wide_rows == wide_lanes, joined, 0.0), axis=1, keepdims=True)
    return (joined * lax.rsqrt(pivots))[:, BLOCK:]


def truncate_kernel(ranks, density, slab, copied, out, work, solved):
    width = density.shape[0]
    copied[...] = slab[...]
    rows = lax.broadcasted_iota(jnp.int32, (width, width), 0)
    lanes = lax.broadcasted_iota(jnp.int32, (width, width), 1)
    identity = jnp.where(rows == lanes, 1.0, 0.0)
    full = identity + density[...] / MEAN
    kept = ranks[lax.axis_index("sec")]
    basis = jnp.where(lanes < kept, full, 0.0)
    basis_t = jnp.where(rows < kept, full, 0.0)
    work[:, :width] = exact_dot(basis_t, basis, ((1,), (0,))) + jnp.where(
        rows < kept, 0.0, identity
    )
    work[:, width:] = basis_t
    for first in range(0, width, BLOCK):
        rest = first + BLOCK
        inverse = inverse_factor(work[first:rest, first:rest])
        reduced = exact_dot(inverse, work[first:rest, :], ((1,), (0,)))
        solved[first:rest, :] = reduced[:, width:]
        if rest < width:
            column = exact_dot(work[rest:, first:rest], inverse, ((1,), (1,)))
            work[rest:, :] = work[rest:, :] - exact_dot(column, reduced, ((1,), (0,)))
    coords = exact_dot(slab[...], solved[...], ((1,), (1,)))
    out[...] = exact_dot(coords, solved[...], ((1,), (0,)))


def truncate(density, slab, ranks):
    width = density.shape[0]
    vmem = pl.BlockSpec(memory_space=pltpu.VMEM)
    return pl.pallas_call(
        truncate_kernel,
        out_shape=(jax.ShapeDtypeStruct(slab.shape, jnp.float32),) * 2,
        in_specs=[pl.BlockSpec(memory_space=pltpu.SMEM), vmem, vmem],
        out_specs=(vmem, vmem),
        scratch_shapes=[
            pltpu.VMEM((width, 2 * width), jnp.float32),
            pltpu.VMEM((width, width), jnp.float32),
        ],
    )(ranks, density, slab)


def shards(guess, left_env, right_env, block_rows, charges, ranks):
    slab, density = iterate(guess, left_env, right_env, block_rows, charges)
    return truncate(density, slab, ranks)


def solution(mesh):
    return jax.shard_map(
        shards,
        mesh=mesh,
        in_specs=(P("sec", None), P("mpo", "sec", None), P("mpo", "sec", None), P(), P("mpo"), P()),
        out_specs=(P(("sec", "mpo"), None), P(("sec", "mpo"), None)),
        check_vma=False,
    )
```

```python
import functools

import jax
import jax.numpy as jnp
from jax import lax
from jax.experimental import pallas as pl
from jax.experimental.pallas import tpu as pltpu
from jax.sharding import PartitionSpec as P

MEAN = 256
ITERS = 4


epsilon = 1e-06
step_size = 0.1
highest = lax.Precision.HIGHEST


PIECES = 2


def row_sum(values):
    return jnp.sum(jnp.sum(values.reshape(-1, 8, 128), axis=0), axis=0, keepdims=True)


def arrival_order(member, members):
    steps = [(-1, 1), (1, -1)][member >= members // 2]
    order = [member]
    for d in range(1, members):
        order += [member + s * d for s in steps if 0 <= member + s * d < members]
    return order


def reduce_order(member, members):
    order = arrival_order(member, members)[1:]
    far = 1 if member < members // 2 else -1
    return sorted(order, key=lambda other: -(abs(other - member) * 2 + ((other - member) * far > 0)))


def tile_order(member, members, tiles):
    return list(range(tiles)) if member < members // 2 else list(range(tiles))[::-1]


def tile_ready(members, tiles):
    ready = [0] * tiles
    for member in range(members):
        order = arrival_order(member, members)
        for i, tile in enumerate(tile_order(member, members, tiles)):
            chunks = range(tile * members // tiles, -(-(tile + 1) * members // tiles))
            ready[i] = max([ready[i]] + [order.index(c) for c in chunks])
    return ready


def transposed_dot(left, right):
    return lax.dot_general(left, right, (((0,), (0,)), ((), ())), preferred_element_type=jnp.float32)


def iterate_kernel(
    sectors, members, entries,
    block_rows, charges, guess, left_hbm, right_hbm, slab, density,
    left, right, xbuf, acc, app_chunk, cur, rs_out, rs_in, scal,
    load_sem, z_s, z_r, n_s, n_r, f_s, f_r, b_s, b_r, p_s, p_r, rs_s, rs_r, sc_s, sc_r,
):
    sector = lax.axis_index("sec")
    member = lax.axis_index("mpo")
    capacity, width = guess.shape
    chunk = capacity // members
    piece = chunk // PIECES
    tiles = left.shape[1]
    terms = left.shape[0]
    chips = sectors // 2
    parity = lax.rem(sector, 2)
    chip = sector // 2
    odd = lax.rem(chip, 2)
    sibling = sector + 1 - 2 * parity
    ahead = lax.rem(sector + 2, sectors)
    behind = lax.rem(sector + sectors - 2, sectors)
    relayed = chips == 4
    interior = jnp.logical_and(member > 0, member < members - 1)
    has_up = member < members - 1
    has_down = member > 0
    always = None
    sends = []

    loads = [pltpu.make_async_copy(right_hbm, right, load_sem.at[tiles])]
    for i in range(tiles):
        loads.append(pltpu.make_async_copy(
            left_hbm.at[:, :, pl.ds(i * width, width)], left.at[:, i], load_sem.at[i]
        ))
    for load in loads:
        load.start()

    barrier = pltpu.get_barrier_semaphore()
    for d in range(1, sectors):
        pl.semaphore_signal(
            barrier, inc=1, device_id=(lax.rem(sector + d, sectors), member),
            device_id_type=pl.DeviceIdType.MESH,
        )
    for d in range(1, members):
        pl.semaphore_signal(
            barrier, inc=1, device_id=(sector, lax.rem(member + d, members)),
            device_id_type=pl.DeviceIdType.MESH,
        )
    pl.semaphore_wait(barrier, sectors + members - 2)

    def remote(src, dst, send, recv, sec, mpo):
        return pltpu.make_async_remote_copy(
            src_ref=src, dst_ref=dst, send_sem=send, recv_sem=recv,
            device_id=(sec, mpo), device_id_type=pl.DeviceIdType.MESH,
        )

    def launch(copy, when=always):
        if when is None:
            copy.start()
        else:
            pl.when(when)(copy.start)
        sends.append((copy, when))

    def by_member(table):
        value = jnp.int32(table[0])
        for m in range(1, members):
            value = jnp.where(member == m, table[m], value)
        return value

    def rows_of(j):
        return pl.ds(pl.multiple_of(j * chunk, chunk), chunk)

    def piece_of(j, q):
        return pl.ds(pl.multiple_of(j * chunk + q * piece, piece), piece)

    order = [by_member([arrival_order(m, members)[r] for m in range(members)]) for r in range(members)]
    targets = [by_member([reduce_order(m, members)[r] for m in range(members)]) for r in range(members - 1)]
    tile_at = [by_member([tile_order(m, members, tiles)[i] for m in range(members)]) for i in range(tiles)]
    ready = tile_ready(members, tiles)

    if relayed:
        near = jnp.where(odd == 1, behind, ahead)
        across = lax.rem(sector + sectors // 2, sectors)
        near_shift = jnp.where(odd == 1, 2, -2)
        pass_near = parity == odd
    else:
        near_shift = jnp.int32(-2)
        pass_near = parity == 0
    far_shift = -near_shift

    def z_send(k, j, q, up, when):
        rows = piece_of(j, q)
        step = 1 if up else -1
        launch(remote(
            xbuf.at[k, 0, rows], xbuf.at[k, 0, rows], z_s.at[k, int(up), j, q], z_r.at[k, j, q],
            sector, jnp.clip(member + step, 0, members - 1),
        ), when)

    def z_forward(k, j, q):
        z_send(k, j, q, True, jnp.logical_and(interior, j < member))
        z_send(k, j, q, False, jnp.logical_and(interior, j > member))

    def near_send(k, j, q):
        rows = piece_of(j, q)
        if relayed:
            launch(remote(
                xbuf.at[k, 0, rows], xbuf.at[k, 2, rows], n_s.at[k, j, q], n_r.at[k, j, q], near, member,
            ))
        else:
            launch(remote(
                xbuf.at[k, 0, rows], xbuf.at[k, 2, rows], n_s.at[k, j, q], n_r.at[k, j, q], behind, member,
            ))
            launch(remote(
                xbuf.at[k, 0, rows], xbuf.at[k, 3, rows], f_s.at[k, j, q], f_r.at[k, j, q], ahead, member,
            ))

    def far_send(k, j, q):
        rows = piece_of(j, q)
        if relayed:
            launch(remote(
                xbuf.at[k, 2, rows], xbuf.at[k, 3, rows], f_s.at[k, j, q], f_r.at[k, j, q], across, member,
            ))

    def sibling_send(k, j):
        rows = rows_of(j)
        launch(remote(
            xbuf.at[k, 0, rows], xbuf.at[k, 1, rows], b_s.at[k, j], b_r.at[k, j], sibling, member,
        ))

    def pass_send(k, j, slot, when):
        rows = rows_of(j)
        launch(remote(
            xbuf.at[k, slot, rows], xbuf.at[k, 4, rows], p_s.at[k, j], p_r.at[k, j], sibling, member,
        ), when)

    def arrived(k, slot, rows, send, recv):
        remote(xbuf.at[k, slot, rows], xbuf.at[k, slot, rows], send, recv, sibling, member).wait_recv()

    def rs_copy(k, r, q):
        return remote(
            rs_out.at[k, r, pl.ds(q * piece, piece)], rs_in.at[k, member, pl.ds(q * piece, piece)],
            rs_s.at[k, r, q], rs_r.at[k, member, q], sector, targets[r],
        )

    def scal_copy(k, d):
        return remote(
            scal.at[k, sector], scal.at[k, sector],
            sc_s.at[k, d - 1], sc_r.at[k, d - 1], lax.rem(sector + d, sectors), member,
        )

    def scal_wait(k):
        for d in range(1, sectors):
            src = lax.rem(sector - d + sectors, sectors)
            remote(
                scal.at[k, src], scal.at[k, src],
                sc_s.at[k, d - 1], sc_r.at[k, d - 1], src, member,
            ).wait_recv()

    def term_of(charge):
        index = jnp.int32(0)
        for i in range(1, terms):
            index = jnp.where(charges[i] == charge, i, index)
        return index

    slot_term = [
        term_of(0), term_of(2 * parity - 1), term_of(near_shift), term_of(far_shift),
        term_of(1 - 2 * parity),
    ]

    def add_tile(k, slot, i, first=False):
        index, tile = slot_term[slot], tile_at[i]
        rows = pl.ds(pl.multiple_of(tile * width, width), width)
        mixed = jnp.dot(
            xbuf[k, slot, rows, :], right[index], preferred_element_type=jnp.float32
        ).astype(jnp.bfloat16)
        value = jnp.dot(left[index, tile], mixed, preferred_element_type=jnp.float32)
        acc[...] = value if first else acc[...] + value

    def send_sums(k, first, second, third):
        rows = [row_sum(first), row_sum(second), row_sum(third), jnp.zeros((5, 128), jnp.float32)]
        scal[k, sector] = jnp.concatenate(rows, axis=0)
        for d in range(1, sectors):
            launch(scal_copy(k, d))

    def coefficients(k):
        sums = jnp.sum(jnp.sum(scal[k], axis=0), axis=1, keepdims=True)
        self_dot, cross_dot, image_dot = sums[0:1], sums[1:2], sums[2:3]
        if k == 0:
            scale = lax.rsqrt(self_dot / entries + epsilon)
            return scale, scale
        rayleigh = cross_dot / (self_dot + epsilon)
        squares = self_dot * (1.0 - (step_size * rayleigh) ** 2) + step_size**2 * image_dot
        scale = lax.rsqrt(squares / entries + epsilon)
        return (1.0 + step_size * rayleigh) * scale, -step_size * scale

    def state_sums(k, keep, add):
        if k == 0:
            send_sums(0, cur[...] * cur[...], jnp.zeros((8, 128)), jnp.zeros((8, 128)))
            return
        if k == 1:
            state = keep * cur[...]
        else:
            state = keep * cur[...] + add * xbuf[k - 1, 0].astype(jnp.float32)
        cur[...] = state
        applied = xbuf[k, 0].astype(jnp.float32)
        send_sums(k, state * state, state * applied, applied * applied)

    own_rows = block_rows[sector]
    positions = lax.broadcasted_iota(jnp.int32, (capacity, width), 0)
    start = jnp.where(positions < own_rows, guess[...], 0.0)
    xbuf[0, 0] = start.astype(jnp.bfloat16)
    cur[...] = start
    keep = add = None

    for k in range(ITERS):
        for r in range(members + 3):
            for q in range(PIECES):
                if r < members:
                    j = order[r]
                    if r > 0 and k > 0:
                        arrived(k, 0, piece_of(j, q), z_s.at[k, 0, j, q], z_r.at[k, j, q])
                        z_forward(k, j, q)
                    if r > 0 or k == 0:
                        near_send(k, j, q)
                if 1 <= r <= members:
                    j = order[r - 1]
                    arrived(k, 2, piece_of(j, q), n_s.at[k, j, q], n_r.at[k, j, q])
                    far_send(k, j, q)
                if 2 <= r <= members + 1:
                    j = order[r - 2]
                    arrived(k, 3, piece_of(j, q), f_s.at[k, j, q], f_r.at[k, j, q])
            if r < members:
                sibling_send(k, order[r])
            if 1 <= r <= members:
                pass_send(k, order[r - 1], 2, pass_near)
            if 2 <= r <= members + 1:
                pass_send(k, order[r - 2], 3, jnp.logical_not(pass_near))
            if r == 0 and k == 0:
                state_sums(0, None, None)
                for load in loads:
                    load.wait()
            for i in range(tiles):
                if ready[i] == r:
                    add_tile(k, 0, i, first=i == 0)
            if 1 <= r <= members:
                j = order[r - 1]
                arrived(k, 1, rows_of(j), b_s.at[k, j], b_r.at[k, j])
            if 3 <= r:
                j = order[r - 3]
                arrived(k, 4, rows_of(j), p_s.at[k, j], p_r.at[k, j])
            for slot, lag in ((1, 1), (2, 1), (3, 2), (4, 3)):
                for i in range(tiles):
                    if ready[i] == r - lag:
                        add_tile(k, slot, i)
            if r == members and k > 0:
                state_sums(k, keep, add)
        for q in range(PIECES):
            for t in range(members - 1):
                rs_out[k, t, pl.ds(q * piece, piece)] = acc[piece_of(targets[t], q), :].astype(jnp.bfloat16)
                launch(rs_copy(k, t, q))
        scal_wait(k)
        keep, add = coefficients(k)
        for q in range(PIECES):
            part = pl.ds(q * piece, piece)
            mine = piece_of(member, q)
            image = acc[mine, :]
            for r in range(1, members):
                j = order[r]
                remote(
                    rs_in.at[k, j, part], rs_in.at[k, j, part],
                    rs_s.at[k, 0, q], rs_r.at[k, j, q], sibling, member,
                ).wait_recv()
                image = image + rs_in[k, j, part].astype(jnp.float32)
            positions = lax.broadcasted_iota(jnp.int32, (piece, width), 0) + member * chunk + q * piece
            image = jnp.where(positions < own_rows, image, 0.0) * add
            if k > 0:
                image = image + keep * app_chunk[part, :]
            app_chunk[part, :] = image
            xbuf[k + 1, 0, mine] = image.astype(jnp.bfloat16)
            z_send(k + 1, member, q, True, has_up)
            z_send(k + 1, member, q, False, has_down)
            if k < ITERS - 1:
                near_send(k + 1, member, q)

    for r in range(1, members):
        for q in range(PIECES):
            j = order[r]
            arrived(ITERS, 0, piece_of(j, q), z_s.at[ITERS, 0, j, q], z_r.at[ITERS, j, q])
            z_forward(ITERS, j, q)
    state_sums(ITERS, keep, add)
    scal_wait(ITERS)
    keep, add = coefficients(ITERS)
    final = keep * cur[...] + add * xbuf[ITERS, 0].astype(jnp.float32)
    cur[...] = final
    slab[...] = cur[rows_of(member), :]
    high = final.astype(jnp.bfloat16)
    low = (final - high.astype(jnp.float32)).astype(jnp.bfloat16)
    mixed = transposed_dot(high, low)
    density[...] = transposed_dot(high, high) + (mixed + mixed.T)
    for copy, when in sends:
        if when is None:
            copy.wait_send()
        else:
            pl.when(when)(copy.wait_send)


def iterate(guess, left_env, right_env, block_rows, charges):
    capacity, width = guess.shape
    terms = left_env.shape[0]
    sectors = lax.axis_size("sec")
    members = lax.axis_size("mpo")
    chunk = capacity // members
    tiles = capacity // width
    entries = MEAN * sectors * width
    dma = pltpu.SemaphoreType.DMA
    vmem = pl.BlockSpec(memory_space=pltpu.VMEM)
    smem = pl.BlockSpec(memory_space=pltpu.SMEM)
    hbm = pl.BlockSpec(memory_space=pl.ANY)
    return pl.pallas_call(
        functools.partial(iterate_kernel, sectors, members, entries),
        out_shape=(
            jax.ShapeDtypeStruct((chunk, width), jnp.float32),
            jax.ShapeDtypeStruct((width, width), jnp.float32),
        ),
        in_specs=[smem, smem, vmem, hbm, hbm],
        out_specs=(vmem, vmem),
        scratch_shapes=[
            pltpu.VMEM((terms, tiles, capacity, width), left_env.dtype),
            pltpu.VMEM((terms, width, width), right_env.dtype),
            pltpu.VMEM((ITERS + 1, 5, capacity, width), jnp.bfloat16),
            pltpu.VMEM((capacity, width), jnp.float32),
            pltpu.VMEM((chunk, width), jnp.float32),
            pltpu.VMEM((capacity, width), jnp.float32),
            pltpu.VMEM((ITERS, members - 1, chunk, width), jnp.bfloat16),
            pltpu.VMEM((ITERS, members, chunk, width), jnp.bfloat16),
            pltpu.VMEM((ITERS + 1, sectors, 8, 128), jnp.float32),
            dma((tiles + 1,)),
            dma((ITERS + 1, 2, members, PIECES)),
            dma((ITERS + 1, members, PIECES)),
            dma((ITERS, members, PIECES)),
            dma((ITERS, members, PIECES)),
            dma((ITERS, members, PIECES)),
            dma((ITERS, members, PIECES)),
            dma((ITERS, members)),
            dma((ITERS, members)),
            dma((ITERS, members)),
            dma((ITERS, members)),
            dma((ITERS, members - 1, PIECES)),
            dma((ITERS, members, PIECES)),
            dma((ITERS + 1, sectors)),
            dma((ITERS + 1, sectors)),
        ],
        compiler_params=pltpu.CompilerParams(
            collective_id=0, has_side_effects=True, vmem_limit_bytes=56 * 1024 * 1024
        ),
    )(block_rows, charges, guess, left_env, right_env)


small_residual = 3e-4


def exact_dot(left, right, dims):
    return lax.dot_general(
        left, right, (dims, ((), ())), precision=highest, preferred_element_type=jnp.float32
    )


def truncate_kernel(ranks, density, slab, copied, out, gram, pair):
    width = density.shape[0]
    copied[...] = slab[...]
    rows = lax.broadcasted_iota(jnp.int32, (width, width), 0)
    lanes = lax.broadcasted_iota(jnp.int32, (width, width), 1)
    identity = jnp.where(rows == lanes, 1.0, 0.0)
    full = identity + density[...] / MEAN
    kept = ranks[lax.axis_index("sec")]
    basis = jnp.where(lanes < kept, full, 0.0)
    basis_t = jnp.where(rows < kept, full, 0.0)
    matrix = exact_dot(basis_t, basis, ((1,), (0,))) + jnp.where(rows < kept, 0.0, identity)
    gram[...] = matrix
    largest = jnp.max(jnp.sum(jnp.abs(matrix), axis=0, keepdims=True))
    scale = 2.0 / (1.0 + largest)
    pair[:width, :] = identity - scale * matrix
    pair[width:, :] = scale * identity

    def unfinished(bound):
        return bound > small_residual

    def step(bound):
        square = bound * bound
        grow = 2.0 / (2.0 - square)
        product = exact_dot(pair[...], pair[:width, :], ((1,), (0,)))
        pair[width:, :] = grow * (pair[width:, :] + product[width:, :])
        pair[:width, :] = (1.0 - grow) * identity + grow * product[:width, :]
        return square / (2.0 - square)

    lax.while_loop(unfinished, step, (largest - 1.0) / (largest + 1.0))
    inverse = pair[width:, :]
    residual = identity - exact_dot(gram[...], inverse, ((1,), (0,)))
    inverse = inverse + exact_dot(inverse, residual, ((1,), (0,)))
    coords = exact_dot(slab[...], basis, ((1,), (0,)))
    solved = exact_dot(coords, inverse, ((1,), (0,)))
    out[...] = exact_dot(solved, basis_t, ((1,), (0,)))


def truncate(density, slab, ranks):
    width = density.shape[0]
    vmem = pl.BlockSpec(memory_space=pltpu.VMEM)
    return pl.pallas_call(
        truncate_kernel,
        out_shape=(jax.ShapeDtypeStruct(slab.shape, jnp.float32),) * 2,
        in_specs=[pl.BlockSpec(memory_space=pltpu.SMEM), vmem, vmem],
        out_specs=(vmem, vmem),
        scratch_shapes=[
            pltpu.VMEM((width, width), jnp.float32),
            pltpu.VMEM((2 * width, width), jnp.float32),
        ],
    )(ranks, density, slab)


def shards(guess, left_env, right_env, block_rows, charges, ranks):
    slab, density = iterate(guess, left_env, right_env, block_rows, charges)
    return truncate(density, slab, ranks)


def solution(mesh):
    return jax.shard_map(
        shards,
        mesh=mesh,
        in_specs=(P("sec", None), P("mpo", "sec", None), P("mpo", "sec", None), P(), P("mpo"), P()),
        out_specs=(P(("sec", "mpo"), None), P(("sec", "mpo"), None)),
        check_vma=False,
    )
```

```python
import functools

import jax
import jax.numpy as jnp
from jax import lax
from jax.experimental import pallas as pl
from jax.experimental.pallas import tpu as pltpu
from jax.sharding import PartitionSpec as P

MEAN = 256
ITERS = 4


epsilon = 1e-06
step_size = 0.1
highest = lax.Precision.HIGHEST


PIECES = 2


def row_sum(values):
    return jnp.sum(jnp.sum(values.reshape(-1, 8, 128), axis=0), axis=0, keepdims=True)


def arrival_order(member, members):
    steps = [(-1, 1), (1, -1)][member >= members // 2]
    order = [member]
    for d in range(1, members):
        order += [member + s * d for s in steps if 0 <= member + s * d < members]
    return order


def reduce_order(member, members):
    order = arrival_order(member, members)[1:]
    far = 1 if member < members // 2 else -1
    return sorted(order, key=lambda other: -(abs(other - member) * 2 + ((other - member) * far > 0)))


def tile_order(member, members, tiles):
    return list(range(tiles)) if member < members // 2 else list(range(tiles))[::-1]


def tile_ready(members, tiles):
    ready = [0] * tiles
    for member in range(members):
        order = arrival_order(member, members)
        for i, tile in enumerate(tile_order(member, members, tiles)):
            chunks = range(tile * members // tiles, -(-(tile + 1) * members // tiles))
            ready[i] = max([ready[i]] + [order.index(c) for c in chunks])
    return ready


def transposed_dot(left, right):
    return lax.dot_general(left, right, (((0,), (0,)), ((), ())), preferred_element_type=jnp.float32)


def iterate_kernel(
    sectors, members, entries, half,
    block_rows, charges, guess, left_hbm, right_hbm, slab, density,
    left, right, xbuf, acc, app_chunk, cur, ex_out, ex_in, rs_out, rs_in, scal,
    load_sem, z_s, z_r, n_s, n_r, f_s, f_r, b_s, b_r, p_s, p_r, e_s, e_r, rs_s, rs_r, sc_s, sc_r,
):
    sector = lax.axis_index("sec")
    member = lax.axis_index("mpo")
    capacity, width = guess.shape
    packed = half < capacity
    shared = 2 * half - capacity
    chunk = half // members
    piece = chunk // PIECES
    depths = left.shape[1]
    tiles = half // width
    terms = left.shape[0]
    chips = sectors // 2
    parity = lax.rem(sector, 2)
    chip = sector // 2
    odd = lax.rem(chip, 2)
    sibling = sector + 1 - 2 * parity
    ahead = lax.rem(sector + 2, sectors)
    behind = lax.rem(sector + sectors - 2, sectors)
    relayed = chips == 4
    interior = jnp.logical_and(member > 0, member < members - 1)
    has_up = member < members - 1
    has_down = member > 0
    always = None
    sends = []

    loads = [pltpu.make_async_copy(right_hbm, right, load_sem.at[depths])]
    for i in range(depths):
        loads.append(pltpu.make_async_copy(
            left_hbm.at[:, :, pl.ds(i * width, width)], left.at[:, i], load_sem.at[i]
        ))
    for load in loads:
        load.start()

    barrier = pltpu.get_barrier_semaphore()
    for d in range(1, sectors):
        pl.semaphore_signal(
            barrier, inc=1, device_id=(lax.rem(sector + d, sectors), member),
            device_id_type=pl.DeviceIdType.MESH,
        )
    for d in range(1, members):
        pl.semaphore_signal(
            barrier, inc=1, device_id=(sector, lax.rem(member + d, members)),
            device_id_type=pl.DeviceIdType.MESH,
        )
    pl.semaphore_wait(barrier, sectors + members - 2)

    def remote(src, dst, send, recv, sec, mpo):
        return pltpu.make_async_remote_copy(
            src_ref=src, dst_ref=dst, send_sem=send, recv_sem=recv,
            device_id=(sec, mpo), device_id_type=pl.DeviceIdType.MESH,
        )

    def launch(copy, when=always):
        if when is None:
            copy.start()
        else:
            pl.when(when)(copy.start)
        sends.append((copy, when))

    def by_member(table):
        value = jnp.int32(table[0])
        for m in range(1, members):
            value = jnp.where(member == m, table[m], value)
        return value

    def rows_of(j):
        return pl.ds(pl.multiple_of(j * chunk, chunk), chunk)

    def piece_of(j, q):
        return pl.ds(pl.multiple_of(j * chunk + q * piece, piece), piece)

    order = [by_member([arrival_order(m, members)[r] for m in range(members)]) for r in range(members)]
    targets = [by_member([reduce_order(m, members)[r] for m in range(members)]) for r in range(members - 1)]
    tile_at = [by_member([tile_order(m, members, tiles)[i] for m in range(members)]) for i in range(tiles)]
    ready = tile_ready(members, tiles)

    if relayed:
        near = jnp.where(odd == 1, behind, ahead)
        across = lax.rem(sector + sectors // 2, sectors)
        near_shift = jnp.where(odd == 1, 2, -2)
        fifth_far = parity == odd
    else:
        near_shift = jnp.int32(-2)
        fifth_far = parity == 0
    far_shift = -near_shift

    def z_send(k, j, q, up, when):
        rows = piece_of(j, q)
        step = 1 if up else -1
        launch(remote(
            xbuf.at[k, 0, rows], xbuf.at[k, 0, rows], z_s.at[k, int(up), j, q], z_r.at[k, j, q],
            sector, jnp.clip(member + step, 0, members - 1),
        ), when)

    def z_forward(k, j, q):
        z_send(k, j, q, True, jnp.logical_and(interior, j < member))
        z_send(k, j, q, False, jnp.logical_and(interior, j > member))

    def near_send(k, j, q):
        rows = piece_of(j, q)
        if relayed:
            launch(remote(
                xbuf.at[k, 0, rows], xbuf.at[k, 2, rows], n_s.at[k, j, q], n_r.at[k, j, q], near, member,
            ))
        else:
            launch(remote(
                xbuf.at[k, 0, rows], xbuf.at[k, 2, rows], n_s.at[k, j, q], n_r.at[k, j, q], behind, member,
            ))
            launch(remote(
                xbuf.at[k, 0, rows], xbuf.at[k, 3, rows], f_s.at[k, j, q], f_r.at[k, j, q], ahead, member,
            ))

    def far_send(k, j, q):
        rows = piece_of(j, q)
        if relayed:
            launch(remote(
                xbuf.at[k, 2, rows], xbuf.at[k, 3, rows], f_s.at[k, j, q], f_r.at[k, j, q], across, member,
            ))

    def sibling_send(k, j):
        rows = rows_of(j)
        launch(remote(
            xbuf.at[k, 0, rows], xbuf.at[k, 1, rows], b_s.at[k, j], b_r.at[k, j], sibling, member,
        ))

    def pass_send(k, j, far):
        rows = rows_of(j)
        launch(remote(
            xbuf.at[k, 2 + far, rows], xbuf.at[k, 4 + far, rows],
            p_s.at[k, far, j], p_r.at[k, far, j], sibling, member,
        ))

    def exchange(k):
        return remote(ex_out.at[k], ex_in.at[k], e_s.at[k], e_r.at[k], sibling, member)

    def arrived(k, slot, rows, send, recv):
        remote(xbuf.at[k, slot, rows], xbuf.at[k, slot, rows], send, recv, sibling, member).wait_recv()

    def rs_copy(k, r, q):
        return remote(
            rs_out.at[k, piece_of(targets[r], q)], rs_in.at[k, member, pl.ds(q * piece, piece)],
            rs_s.at[k, r, q], rs_r.at[k, member, q], sector, targets[r],
        )

    def scal_copy(k, d):
        return remote(
            scal.at[k, sector], scal.at[k, sector],
            sc_s.at[k, d - 1], sc_r.at[k, d - 1], lax.rem(sector + d, sectors), member,
        )

    def scal_wait(k):
        for d in range(1, sectors):
            src = lax.rem(sector - d + sectors, sectors)
            remote(
                scal.at[k, src], scal.at[k, src],
                sc_s.at[k, d - 1], sc_r.at[k, d - 1], src, member,
            ).wait_recv()

    def term_of(charge):
        index = jnp.int32(0)
        for i in range(1, terms):
            index = jnp.where(charges[i] == charge, i, index)
        return index

    def count_of(shift):
        return block_rows[lax.rem(sector + shift + sectors, sectors)]

    own_rows, sibling_rows = count_of(0), block_rows[sibling]
    fifth = 2 * parity - 1
    both_far = jnp.where(fifth_far, 1, 0)
    term_own, term_sibling = term_of(0), term_of(2 * parity - 1)
    term_near, term_far, term_fifth = term_of(near_shift), term_of(far_shift), term_of(-fifth)

    def over(rows):
        return jnp.where(rows > half, 1, 0)

    mates = 1 - 2 * parity
    fifth_slot, other_slot = 4 + both_far, 5 - both_far
    fifth_mate = jnp.where(fifth_far, term_far, term_near)
    other_mate = jnp.where(fifth_far, term_near, term_far)
    far_rows, near_rows = count_of(-far_shift), count_of(-near_shift)
    near_tail = over(count_of(-near_shift + mates))
    far_tail = over(count_of(-far_shift + mates))
    tasks = {
        0: (0, term_own, term_sibling, over(sibling_rows), 1),
        1: (1, term_sibling, term_own, over(own_rows), 1),
        2: (2, term_near, term_fifth, near_tail, 1 - both_far),
        3: (3, term_far, term_fifth, far_tail, both_far),
        4: (fifth_slot, term_fifth, fifth_mate, over(jnp.where(fifth_far, far_rows, near_rows)), 1),
    }
    other_tail = over(jnp.where(fifth_far, near_rows, far_rows))

    def product(k, slot, start, index, depth, keep_rows, rows):
        value = xbuf[k, slot, pl.ds(pl.multiple_of(start, width), width), :]
        if keep_rows is not None:
            value = jnp.where(keep_rows > 0, value, jnp.zeros_like(value))
        mixed = jnp.dot(value, right[index], preferred_element_type=jnp.float32).astype(jnp.bfloat16)
        return jnp.dot(left[index, depth, rows, :], mixed, preferred_element_type=jnp.float32)

    everything = pl.ds(0, capacity)

    def add_tile(k, group, i, first=False, rows=everything):
        slot, index, mate, tail, counted = tasks[group]
        depth, keep_rows = tile_at[i], None
        start = depth * width
        if packed:
            ends = jnp.where(start >= shared, tail, 0)
            index = jnp.where(ends > 0, mate, index)
            depth = jnp.where(ends > 0, depth + (half - shared) // width, depth)
            keep_rows = 1 - ends * (1 - counted)
        value = product(k, slot, start, index, depth, keep_rows, rows)
        acc[rows, :] = value if first else acc[rows, :] + value

    def add_other(k, rows=everything):
        for i in range(shared // width, tiles):
            depth = i + (half - shared) // width
            acc[rows, :] = acc[rows, :] + product(
                k, other_slot, i * width, other_mate, depth, other_tail, rows
            )

    def block(k):
        if not packed:
            return xbuf[k, 0].astype(jnp.float32)
        ending = xbuf[k, 0, pl.ds(shared, half - shared), :]
        beyond = xbuf[k, 1, pl.ds(shared, half - shared), :]
        return jnp.concatenate([
            xbuf[k, 0, pl.ds(0, shared), :],
            jnp.where(sibling_rows > half, jnp.zeros_like(ending), ending),
            jnp.where(own_rows > half, beyond, jnp.zeros_like(beyond)),
        ], axis=0).astype(jnp.float32)

    def send_sums(k, first, second, third):
        rows = [row_sum(first), row_sum(second), row_sum(third), jnp.zeros((5, 128), jnp.float32)]
        scal[k, sector] = jnp.concatenate(rows, axis=0)
        for d in range(1, sectors):
            launch(scal_copy(k, d))

    def coefficients(k):
        sums = jnp.sum(jnp.sum(scal[k], axis=0), axis=1, keepdims=True)
        self_dot, cross_dot, image_dot = sums[0:1], sums[1:2], sums[2:3]
        if k == 0:
            scale = lax.rsqrt(self_dot / entries + epsilon)
            return scale, scale
        rayleigh = cross_dot / (self_dot + epsilon)
        squares = self_dot * (1.0 - (step_size * rayleigh) ** 2) + step_size**2 * image_dot
        scale = lax.rsqrt(squares / entries + epsilon)
        return (1.0 + step_size * rayleigh) * scale, -step_size * scale

    def state_sums(k, keep, add):
        if k == 0:
            send_sums(0, cur[...] * cur[...], jnp.zeros((8, 128)), jnp.zeros((8, 128)))
            return
        if k == 1:
            state = keep * cur[...]
        else:
            state = keep * cur[...] + add * block(k - 1)
        cur[...] = state
        applied = block(k)
        send_sums(k, state * state, state * applied, applied * applied)

    def pack(k, target):
        if packed:
            ending = target[pl.ds(shared, half - shared), :]
            exchange(k).wait_recv()
            target[pl.ds(shared, half - shared), :] = jnp.where(sibling_rows > half, ex_in[k], ending)

    def offer(k, rows):
        if packed:
            ex_out[k] = rows
            launch(exchange(k))

    positions = lax.broadcasted_iota(jnp.int32, (capacity, width), 0)
    start = jnp.where(positions < own_rows, guess[...], 0.0)
    cur[...] = start
    offer(ITERS, cur[pl.ds(half, capacity - half), :].astype(jnp.bfloat16) if packed else None)
    xbuf[0, 0] = cur[pl.ds(0, half), :].astype(jnp.bfloat16)
    pack(ITERS, xbuf.at[0, 0])
    keep = add = None
    rounds = members + 3
    borrowed = jnp.logical_and(sibling_rows > half, member * chunk >= shared) if packed else None

    for k in range(ITERS):
        for r in range(rounds):
            for q in range(PIECES):
                if r < members:
                    j = order[r]
                    if r > 0 and k > 0:
                        arrived(k, 0, piece_of(j, q), z_s.at[k, 0, j, q], z_r.at[k, j, q])
                        z_forward(k, j, q)
                    if r > 0 or k == 0:
                        near_send(k, j, q)
                if 1 <= r <= members:
                    j = order[r - 1]
                    arrived(k, 2, piece_of(j, q), n_s.at[k, j, q], n_r.at[k, j, q])
                    far_send(k, j, q)
                if 2 <= r <= members + 1:
                    j = order[r - 2]
                    arrived(k, 3, piece_of(j, q), f_s.at[k, j, q], f_r.at[k, j, q])
            if r < members:
                sibling_send(k, order[r])
            if 1 <= r <= members:
                pass_send(k, order[r - 1], 0)
            if 2 <= r <= members + 1:
                pass_send(k, order[r - 2], 1)
            if r == 0 and k == 0:
                state_sums(0, None, None)
                for load in loads:
                    load.wait()
            for i in range(tiles):
                if ready[i] == r:
                    add_tile(k, 0, i, first=i == 0)
            if 1 <= r <= members:
                j = order[r - 1]
                arrived(k, 1, rows_of(j), b_s.at[k, j], b_r.at[k, j])
            if 2 <= r <= members + 1:
                j = order[r - 2]
                arrived(k, 4, rows_of(j), p_s.at[k, 0, j], p_r.at[k, 0, j])
            if 3 <= r:
                j = order[r - 3]
                arrived(k, 5, rows_of(j), p_s.at[k, 1, j], p_r.at[k, 1, j])
            if r == rounds - 1 and packed:
                ranges = (pl.ds(half, capacity - half), pl.ds(0, half))
            else:
                ranges = (everything,)
            for rows in ranges:
                for group, lag in ((1, 1), (2, 1), (3, 2), (4, 3)):
                    for i in range(tiles):
                        if ready[i] == r - lag:
                            add_tile(k, group, i, rows=rows)
                if r == rounds - 1 and packed:
                    add_other(k, rows)
                    if rows is ranges[0]:
                        offer(k, acc[rows, :].astype(jnp.bfloat16))
            if r == members and k > 0:
                state_sums(k, keep, add)
        rs_out[k] = acc[pl.ds(0, half), :].astype(jnp.bfloat16)
        pack(k, rs_out.at[k])
        for q in range(PIECES):
            for t in range(members - 1):
                launch(rs_copy(k, t, q))
        scal_wait(k)
        keep, add = coefficients(k)
        for q in range(PIECES):
            part = pl.ds(q * piece, piece)
            mine = piece_of(member, q)
            image = acc[mine, :]
            first, limit = member * chunk + q * piece, own_rows
            if packed:
                lent = pl.multiple_of(jnp.maximum(member * chunk - shared, 0) + q * piece, piece)
                image = jnp.where(borrowed, ex_in[k, pl.ds(lent, piece), :].astype(jnp.float32), image)
                first = jnp.where(borrowed, first - shared + half, first)
                limit = jnp.where(borrowed, sibling_rows, limit)
            for r in range(1, members):
                j = order[r]
                remote(
                    rs_in.at[k, j, part], rs_in.at[k, j, part],
                    rs_s.at[k, 0, q], rs_r.at[k, j, q], sibling, member,
                ).wait_recv()
                image = image + rs_in[k, j, part].astype(jnp.float32)
            positions = lax.broadcasted_iota(jnp.int32, (piece, width), 0) + first
            image = jnp.where(positions < limit, image, 0.0) * add
            if k > 0:
                image = image + keep * app_chunk[part, :]
            app_chunk[part, :] = image
            xbuf[k + 1, 0, mine] = image.astype(jnp.bfloat16)
            z_send(k + 1, member, q, True, has_up)
            z_send(k + 1, member, q, False, has_down)
            if k < ITERS - 1:
                near_send(k + 1, member, q)

    for r in range(members):
        j = order[r]
        for q in range(PIECES):
            if r > 0:
                arrived(ITERS, 0, piece_of(j, q), z_s.at[ITERS, 0, j, q], z_r.at[ITERS, j, q])
                z_forward(ITERS, j, q)
        if packed:
            sibling_send(ITERS, j)
    if packed:
        for j in order:
            arrived(ITERS, 1, rows_of(j), b_s.at[ITERS, j], b_r.at[ITERS, j])
    state_sums(ITERS, keep, add)
    scal_wait(ITERS)
    keep, add = coefficients(ITERS)
    final = keep * cur[...] + add * block(ITERS)
    cur[...] = final
    slab_rows = capacity // members
    slab[...] = cur[pl.ds(pl.multiple_of(member * slab_rows, slab_rows), slab_rows), :]
    high = final.astype(jnp.bfloat16)
    low = (final - high.astype(jnp.float32)).astype(jnp.bfloat16)
    mixed = transposed_dot(high, low)
    density[...] = transposed_dot(high, high) + (mixed + mixed.T)
    for copy, when in sends:
        if when is None:
            copy.wait_send()
        else:
            pl.when(when)(copy.wait_send)


def iterate(half, guess, left_env, right_env, block_rows, charges):
    capacity, width = guess.shape
    terms = left_env.shape[0]
    sectors = lax.axis_size("sec")
    members = lax.axis_size("mpo")
    chunk = half // members
    depths = capacity // width
    lent = max(capacity - half, 16)
    entries = MEAN * sectors * width
    dma = pltpu.SemaphoreType.DMA
    vmem = pl.BlockSpec(memory_space=pltpu.VMEM)
    smem = pl.BlockSpec(memory_space=pltpu.SMEM)
    hbm = pl.BlockSpec(memory_space=pl.ANY)
    return pl.pallas_call(
        functools.partial(iterate_kernel, sectors, members, entries, half),
        out_shape=(
            jax.ShapeDtypeStruct((capacity // members, width), jnp.float32),
            jax.ShapeDtypeStruct((width, width), jnp.float32),
        ),
        in_specs=[smem, smem, vmem, hbm, hbm],
        out_specs=(vmem, vmem),
        scratch_shapes=[
            pltpu.VMEM((terms, depths, capacity, width), left_env.dtype),
            pltpu.VMEM((terms, width, width), right_env.dtype),
            pltpu.VMEM((ITERS + 1, 6, half, width), jnp.bfloat16),
            pltpu.VMEM((capacity, width), jnp.float32),
            pltpu.VMEM((chunk, width), jnp.float32),
            pltpu.VMEM((capacity, width), jnp.float32),
            pltpu.VMEM((ITERS + 1, lent, width), jnp.bfloat16),
            pltpu.VMEM((ITERS + 1, lent, width), jnp.bfloat16),
            pltpu.VMEM((ITERS, half, width), jnp.bfloat16),
            pltpu.VMEM((ITERS, members, chunk, width), jnp.bfloat16),
            pltpu.VMEM((ITERS + 1, sectors, 8, 128), jnp.float32),
            dma((depths + 1,)),
            dma((ITERS + 1, 2, members, PIECES)),
            dma((ITERS + 1, members, PIECES)),
            dma((ITERS, members, PIECES)),
            dma((ITERS, members, PIECES)),
            dma((ITERS, members, PIECES)),
            dma((ITERS, members, PIECES)),
            dma((ITERS + 1, members)),
            dma((ITERS + 1, members)),
            dma((ITERS, 2, members)),
            dma((ITERS, 2, members)),
            dma((ITERS + 1,)),
            dma((ITERS + 1,)),
            dma((ITERS, members - 1, PIECES)),
            dma((ITERS, members, PIECES)),
            dma((ITERS + 1, sectors)),
            dma((ITERS + 1, sectors)),
        ],
        compiler_params=pltpu.CompilerParams(
            collective_id=0 if half < capacity else 1,
            has_side_effects=True, vmem_limit_bytes=56 * 1024 * 1024,
        ),
    )(block_rows, charges, guess, left_env, right_env)


small_residual = 3e-4


def exact_dot(left, right, dims):
    return lax.dot_general(
        left, right, (dims, ((), ())), precision=highest, preferred_element_type=jnp.float32
    )


def truncate_kernel(ranks, density, slab, copied, out, gram, pair):
    width = density.shape[0]
    copied[...] = slab[...]
    rows = lax.broadcasted_iota(jnp.int32, (width, width), 0)
    lanes = lax.broadcasted_iota(jnp.int32, (width, width), 1)
    identity = jnp.where(rows == lanes, 1.0, 0.0)
    full = identity + density[...] / MEAN
    kept = ranks[lax.axis_index("sec")]
    basis = jnp.where(lanes < kept, full, 0.0)
    basis_t = jnp.where(rows < kept, full, 0.0)
    matrix = exact_dot(basis_t, basis, ((1,), (0,))) + jnp.where(rows < kept, 0.0, identity)
    gram[...] = matrix
    largest = jnp.max(jnp.sum(jnp.abs(matrix), axis=0, keepdims=True))
    scale = 2.0 / (1.0 + largest)
    pair[:width, :] = identity - scale * matrix
    pair[width:, :] = scale * identity

    def unfinished(bound):
        return bound > small_residual

    def step(bound):
        square = bound * bound
        grow = 2.0 / (2.0 - square)
        product = exact_dot(pair[...], pair[:width, :], ((1,), (0,)))
        pair[width:, :] = grow * (pair[width:, :] + product[width:, :])
        pair[:width, :] = (1.0 - grow) * identity + grow * product[:width, :]
        return square / (2.0 - square)

    lax.while_loop(unfinished, step, (largest - 1.0) / (largest + 1.0))
    inverse = pair[width:, :]
    coords = exact_dot(slab[...], basis, ((1,), (0,)))
    solved = exact_dot(coords, inverse, ((1,), (0,)))
    rest = coords - exact_dot(solved, gram[...], ((1,), (0,)))
    solved = solved + exact_dot(rest, inverse, ((1,), (0,)))
    out[...] = exact_dot(solved, basis_t, ((1,), (0,)))


def truncate(density, slab, ranks):
    width = density.shape[0]
    vmem = pl.BlockSpec(memory_space=pltpu.VMEM)
    return pl.pallas_call(
        truncate_kernel,
        out_shape=(jax.ShapeDtypeStruct(slab.shape, jnp.float32),) * 2,
        in_specs=[pl.BlockSpec(memory_space=pltpu.SMEM), vmem, vmem],
        out_specs=(vmem, vmem),
        scratch_shapes=[
            pltpu.VMEM((width, width), jnp.float32),
            pltpu.VMEM((2 * width, width), jnp.float32),
        ],
    )(ranks, density, slab)


def shards(guess, left_env, right_env, block_rows, charges, ranks):
    capacity, width = guess.shape
    half = capacity - width
    shared = 2 * half - capacity
    first, second = block_rows[0::2], block_rows[1::2]
    most, least = jnp.maximum(first, second), jnp.minimum(first, second)
    fits = jnp.all(jnp.logical_or(most <= half, least <= shared))
    slab, density = lax.cond(
        fits, functools.partial(iterate, half), functools.partial(iterate, capacity),
        guess, left_env, right_env, block_rows, charges,
    )
    return truncate(density, slab, ranks)


def solution(mesh):
    return jax.shard_map(
        shards,
        mesh=mesh,
        in_specs=(P("sec", None), P("mpo", "sec", None), P("mpo", "sec", None), P(), P("mpo"), P()),
        out_specs=(P(("sec", "mpo"), None), P(("sec", "mpo"), None)),
        check_vma=False,
    )
```

```python
import functools

import jax
import jax.numpy as jnp
from jax import lax
from jax.experimental import pallas as pl
from jax.experimental.pallas import tpu as pltpu
from jax.sharding import PartitionSpec as P

MEAN = 256
ITERS = 4


epsilon = 1e-06
step_size = 0.1
highest = lax.Precision.HIGHEST


def row_sum(values):
    return jnp.sum(jnp.sum(values.reshape(-1, 8, 128), axis=0), axis=0, keepdims=True)


def arrival_order(member, members):
    steps = [(-1, 1), (1, -1)][member >= members // 2]
    order = [member]
    for d in range(1, members):
        order += [member + s * d for s in steps if 0 <= member + s * d < members]
    return order


def reduce_order(member, members):
    order = arrival_order(member, members)[1:]
    far = 1 if member < members // 2 else -1
    return sorted(order, key=lambda other: -(abs(other - member) * 2 + ((other - member) * far > 0)))


def transposed_dot(left, right):
    return lax.dot_general(left, right, (((0,), (0,)), ((), ())), preferred_element_type=jnp.float32)


def iterate_kernel(
    sectors, members, entries, half,
    block_rows, charges, guess, left_hbm, right_hbm, slab, density,
    left, right, xbuf, acc, app_chunk, cur, ex_out, ex_in, rs_out, rs_in, scal,
    load_sem, z_s, z_r, n_s, n_r, f_s, f_r, b_s, b_r, p_s, p_r, e_s, e_r, rs_s, rs_r, sc_s, sc_r,
):
    sector = lax.axis_index("sec")
    member = lax.axis_index("mpo")
    capacity, width = guess.shape
    packed = half < capacity
    shared = 2 * half - capacity
    tiles = half // width
    piece = width // members
    depths = left.shape[1]
    terms = left.shape[0]
    chips = sectors // 2
    parity = lax.rem(sector, 2)
    chip = sector // 2
    odd = lax.rem(chip, 2)
    sibling = sector + 1 - 2 * parity
    ahead = lax.rem(sector + 2, sectors)
    behind = lax.rem(sector + sectors - 2, sectors)
    square = chips == 4
    sends = []

    loads = [pltpu.make_async_copy(right_hbm, right, load_sem.at[depths])]
    for i in range(depths):
        loads.append(pltpu.make_async_copy(
            left_hbm.at[:, :, pl.ds(i * width, width)], left.at[:, i], load_sem.at[i]
        ))
    for load in loads:
        load.start()

    barrier = pltpu.get_barrier_semaphore()
    for d in range(1, sectors):
        pl.semaphore_signal(
            barrier, inc=1, device_id=(lax.rem(sector + d, sectors), member),
            device_id_type=pl.DeviceIdType.MESH,
        )
    for d in range(1, members):
        pl.semaphore_signal(
            barrier, inc=1, device_id=(sector, lax.rem(member + d, members)),
            device_id_type=pl.DeviceIdType.MESH,
        )
    pl.semaphore_wait(barrier, sectors + members - 2)

    def remote(src, dst, send, recv, sec, mpo):
        return pltpu.make_async_remote_copy(
            src_ref=src, dst_ref=dst, send_sem=send, recv_sem=recv,
            device_id=(sec, mpo), device_id_type=pl.DeviceIdType.MESH,
        )

    def launch(copy):
        copy.start()
        sends.append(copy)

    def by_member(table):
        value = jnp.int32(table[0])
        for m in range(1, members):
            value = jnp.where(member == m, table[m], value)
        return value

    def tile_rows(q):
        return pl.ds(q * width, width)

    def piece_of(j, q):
        return pl.ds(pl.multiple_of(q * width + j * piece, piece), piece)

    order = [by_member([arrival_order(m, members)[r] for m in range(members)]) for r in range(members)]
    targets = [by_member([reduce_order(m, members)[r] for m in range(members)]) for r in range(members - 1)]
    if square:
        near = jnp.where(odd == 1, behind, ahead)
        across = lax.rem(sector + sectors // 2, sectors)
        distant = jnp.where(odd == 1, ahead, behind)
        near_shift = jnp.where(odd == 1, 2, -2)
        fifth_far = parity == odd
    else:
        near, distant = behind, ahead
        near_shift = jnp.int32(-2)
        fifth_far = parity == 0
    far_shift = -near_shift

    def z_send(k, t, q):
        rows = piece_of(member, q)
        launch(remote(
            xbuf.at[k, 0, rows], xbuf.at[k, 0, rows], z_s.at[k, t, q], z_r.at[k, member, q],
            sector, targets[t],
        ))

    def z_wait(k, j, q):
        arrived(k, 0, piece_of(j, q), z_s.at[k, 0, q], z_r.at[k, j, q])

    def near_send(k, j, q):
        rows = piece_of(j, q)
        launch(remote(
            xbuf.at[k, 0, rows], xbuf.at[k, 2, rows], n_s.at[k, j, q], n_r.at[k, j, q], near, member,
        ))

    def far_send(k, j, q):
        rows = piece_of(j, q)
        launch(remote(
            xbuf.at[k, 0, rows], xbuf.at[k, 3, rows], f_s.at[k, j, q], f_r.at[k, j, q], distant, member,
        ))

    def far_relay(k, j, q):
        rows = piece_of(j, q)
        launch(remote(
            xbuf.at[k, 2, rows], xbuf.at[k, 3, rows], f_s.at[k, j, q], f_r.at[k, j, q], across, member,
        ))

    def sibling_send(k, q):
        rows = tile_rows(q)
        launch(remote(
            xbuf.at[k, 0, rows], xbuf.at[k, 1, rows], b_s.at[k, q], b_r.at[k, q], sibling, member,
        ))

    def pass_send(k, q, far):
        rows = tile_rows(q)
        launch(remote(
            xbuf.at[k, 2 + far, rows], xbuf.at[k, 4 + far, rows],
            p_s.at[k, far, q], p_r.at[k, far, q], sibling, member,
        ))

    def exchange(k):
        return remote(ex_out.at[k], ex_in.at[k], e_s.at[k], e_r.at[k], sibling, member)

    def arrived(k, slot, rows, send, recv):
        remote(xbuf.at[k, slot, rows], xbuf.at[k, slot, rows], send, recv, sibling, member).wait_recv()

    def rs_copy(k, t, q):
        return remote(
            rs_out.at[k, piece_of(targets[t], q)], rs_in.at[k, member, pl.ds(q * piece, piece)],
            rs_s.at[k, t, q], rs_r.at[k, member, q], sector, targets[t],
        )

    def scal_copy(k, d):
        return remote(
            scal.at[k, sector], scal.at[k, sector],
            sc_s.at[k, d - 1], sc_r.at[k, d - 1], lax.rem(sector + d, sectors), member,
        )

    def scal_wait(k):
        for d in range(1, sectors):
            src = lax.rem(sector - d + sectors, sectors)
            remote(
                scal.at[k, src], scal.at[k, src],
                sc_s.at[k, d - 1], sc_r.at[k, d - 1], src, member,
            ).wait_recv()

    def term_of(charge):
        index = jnp.int32(0)
        for i in range(1, terms):
            index = jnp.where(charges[i] == charge, i, index)
        return index

    def count_of(shift):
        return block_rows[lax.rem(sector + shift + sectors, sectors)]

    own_rows, sibling_rows = count_of(0), block_rows[sibling]
    fifth = 2 * parity - 1
    both_far = jnp.where(fifth_far, 1, 0)
    term_own, term_sibling = term_of(0), term_of(2 * parity - 1)
    term_near, term_far, term_fifth = term_of(near_shift), term_of(far_shift), term_of(-fifth)

    def over(rows):
        return jnp.where(rows > half, 1, 0)

    mates = 1 - 2 * parity
    fifth_slot = 4 + both_far
    far_rows, near_rows = count_of(-far_shift), count_of(-near_shift)
    near_tail = over(count_of(-near_shift + mates))
    far_tail = over(count_of(-far_shift + mates))
    tasks = {
        0: (0, term_own, term_sibling, over(sibling_rows), 1),
        1: (1, term_sibling, term_own, over(own_rows), 1),
        2: (2, term_near, term_fifth, near_tail, 1 - both_far),
        3: (3, term_far, term_fifth, far_tail, both_far),
        4: (fifth_slot, term_fifth, term_fifth, 0, 1),
    }
    ends = (
        (term_near, over(near_rows), 1 - both_far), (term_far, over(far_rows), both_far),
    )

    def mix(k, slot, q, index, keep_rows=None):
        value = xbuf[k, slot, tile_rows(q), :]
        if keep_rows is not None:
            value = jnp.where(keep_rows > 0, value, jnp.zeros_like(value))
        return jnp.dot(value, right[index], preferred_element_type=jnp.float32).astype(jnp.bfloat16)

    def tile_task(k, group, q):
        slot, index, mate, tail, counted = tasks[group]
        depth, keep_rows = q, None
        if packed and q * width >= shared:
            index = jnp.where(tail > 0, mate, index)
            depth = jnp.where(tail > 0, q + (half - shared) // width, q)
            keep_rows = 1 - tail * (1 - counted)
        return index, depth, mix(k, slot, q, index, keep_rows)

    def passed_task(k, q, far):
        index, tail, counted = ends[far]
        index = jnp.where(tail > 0, index, term_fifth)
        depth = jnp.where(tail > 0, q + (half - shared) // width, q)
        return index, depth, mix(k, 4 + far, q, index, jnp.maximum(tail, counted))

    def add(task, rows=pl.ds(0, capacity), first=False):
        index, depth, mixed = task
        value = jnp.dot(left[index, depth, rows, :], mixed, preferred_element_type=jnp.float32)
        acc[rows, :] = value if first else acc[rows, :] + value

    def block(k):
        if not packed:
            return xbuf[k, 0].astype(jnp.float32)
        ending = xbuf[k, 0, pl.ds(shared, half - shared), :]
        beyond = xbuf[k, 1, pl.ds(shared, half - shared), :]
        return jnp.concatenate([
            xbuf[k, 0, pl.ds(0, shared), :],
            jnp.where(sibling_rows > half, jnp.zeros_like(ending), ending),
            jnp.where(own_rows > half, beyond, jnp.zeros_like(beyond)),
        ], axis=0).astype(jnp.float32)

    def send_sums(k, first, second, third):
        rows = [row_sum(first), row_sum(second), row_sum(third), jnp.zeros((5, 128), jnp.float32)]
        scal[k, sector] = jnp.concatenate(rows, axis=0)
        for d in range(1, sectors):
            launch(scal_copy(k, d))

    def coefficients(k):
        sums = jnp.sum(jnp.sum(scal[k], axis=0), axis=1, keepdims=True)
        self_dot, cross_dot, image_dot = sums[0:1], sums[1:2], sums[2:3]
        if k == 0:
            scale = lax.rsqrt(self_dot / entries + epsilon)
            return scale, scale
        rayleigh = cross_dot / (self_dot + epsilon)
        squares = self_dot * (1.0 - (step_size * rayleigh) ** 2) + step_size**2 * image_dot
        scale = lax.rsqrt(squares / entries + epsilon)
        return (1.0 + step_size * rayleigh) * scale, -step_size * scale

    def state_sums(k, keep, gain):
        if k == 0:
            send_sums(0, cur[...] * cur[...], jnp.zeros((8, 128)), jnp.zeros((8, 128)))
            return
        if k == 1:
            state = keep * cur[...]
        else:
            state = keep * cur[...] + gain * block(k - 1)
        cur[...] = state
        applied = block(k)
        send_sums(k, state * state, state * applied, applied * applied)

    def pack(k, q, rows):
        if not packed or q * width < shared:
            return rows
        if q * width == shared:
            exchange(k).wait_recv()
        return jnp.where(sibling_rows > half, ex_in[k, pl.ds(q * width - shared, width), :], rows)

    def offer(k, rows):
        ex_out[k] = rows.astype(jnp.bfloat16)
        launch(exchange(k))

    positions = lax.broadcasted_iota(jnp.int32, (capacity, width), 0)
    start = jnp.where(positions < own_rows, guess[...], 0.0)
    cur[...] = start
    if packed:
        offer(ITERS, cur[pl.ds(half, capacity - half), :])
    for q in range(tiles):
        xbuf[0, 0, tile_rows(q)] = pack(ITERS, q, cur[tile_rows(q), :].astype(jnp.bfloat16))
        for j in range(members):
            near_send(0, j, q)
            if not square:
                far_send(0, j, q)
        sibling_send(0, q)
    keep = gain = None

    def near_tile(k, q):
        for j in order:
            arrived(k, 2, piece_of(j, q), n_s.at[k, j, q], n_r.at[k, j, q])
            if k == 0 and square:
                far_relay(k, j, q)
        pass_send(k, q, 0)

    def far_tile(k, q):
        for j in order:
            arrived(k, 3, piece_of(j, q), f_s.at[k, j, q], f_r.at[k, j, q])
        pass_send(k, q, 1)

    def sibling_tile(k, q):
        arrived(k, 1, tile_rows(q), b_s.at[k, q], b_r.at[k, q])

    def passed_tile(k, q, far):
        arrived(k, 4 + far, tile_rows(q), p_s.at[k, far, q], p_r.at[k, far, q])

    def gather(k):
        for q in range(tiles):
            for j in order[1:]:
                z_wait(k, j, q)
                if k < ITERS:
                    far_send(k, j, q)
                    near_send(k, j, q)
            sibling_send(k, q)
            if k < ITERS:
                add(tile_task(k, 0, q), first=q == 0)

    for k in range(ITERS):
        if k == 0:
            state_sums(0, None, None)
            for load in loads:
                load.wait()
        if k == 0:
            for q in range(tiles):
                add(tile_task(k, 0, q), first=q == 0)
        else:
            gather(k)
        for q in range(tiles):
            for p in (q,) if k > 0 else range(tiles) if q == 0 else ():
                near_tile(k, p)
            add(tile_task(k, 2, q))
            far_tile(k, q)
            if q == tiles - 1:
                passed_tile(k, q, 0)
                if packed:
                    add(passed_task(k, q, 0))
            add(tile_task(k, 3, q))
            if q == 0:
                for i in range(tiles):
                    sibling_tile(k, i)
                    add(tile_task(k, 1, i))
                if k > 0:
                    state_sums(k, keep, gain)
            if q < tiles - 1:
                passed_tile(k, q, 0)
                passed_tile(k, q, 1)
                if packed and q * width >= shared:
                    add(passed_task(k, q, 0))
                    add(passed_task(k, q, 1))
                else:
                    add(tile_task(k, 4, q))
        passed_tile(k, tiles - 1, 1)
        if packed:
            last = passed_task(k, tiles - 1, 1)
            rows = pl.ds(half, capacity - half)
            add(last, rows)
            offer(k, acc[rows, :])
        else:
            last = tile_task(k, 4, tiles - 1)
        for q in range(tiles):
            add(last, tile_rows(q))
            rs_out[k, tile_rows(q)] = pack(k, q, acc[tile_rows(q), :].astype(jnp.bfloat16))
            for t in range(members - 1):
                launch(rs_copy(k, t, q))
        scal_wait(k)
        keep, gain = coefficients(k)
        for q in range(tiles):
            part = pl.ds(q * piece, piece)
            mine = piece_of(member, q)
            image = acc[mine, :]
            first, limit = member * piece + q * width, own_rows
            if packed and q * width >= shared:
                borrowed = sibling_rows > half
                lent = pl.ds(pl.multiple_of(q * width - shared + member * piece, piece), piece)
                image = jnp.where(borrowed, ex_in[k, lent, :].astype(jnp.float32), image)
                first = jnp.where(borrowed, first - shared + half, first)
                limit = jnp.where(borrowed, sibling_rows, limit)
            for j in order[1:]:
                remote(
                    rs_in.at[k, j, part], rs_in.at[k, j, part],
                    rs_s.at[k, 0, q], rs_r.at[k, j, q], sibling, member,
                ).wait_recv()
                image = image + rs_in[k, j, part].astype(jnp.float32)
            positions = lax.broadcasted_iota(jnp.int32, (piece, width), 0) + first
            image = jnp.where(positions < limit, image, 0.0) * gain
            if k > 0:
                image = image + keep * app_chunk[part, :]
            app_chunk[part, :] = image
            xbuf[k + 1, 0, mine] = image.astype(jnp.bfloat16)
            for t in reversed(range(members - 1)):
                z_send(k + 1, t, q)
            if k < ITERS - 1:
                far_send(k + 1, member, q)
                near_send(k + 1, member, q)

    state = keep * cur[...] + gain * block(ITERS - 1)
    cur[...] = state
    high = state.astype(jnp.bfloat16)
    low = (state - high.astype(jnp.float32)).astype(jnp.bfloat16)
    mixed = transposed_dot(high, low)
    density[...] = transposed_dot(high, high) + (mixed + mixed.T)
    gather(ITERS)
    for q in range(tiles):
        sibling_tile(ITERS, q)
    applied = block(ITERS)
    send_sums(ITERS, state * state, state * applied, applied * applied)
    final_step = applied.astype(jnp.bfloat16)
    crossed = transposed_dot(high, final_step) + transposed_dot(low, final_step)
    crossed = crossed + crossed.T
    squared = transposed_dot(final_step, final_step)
    scal_wait(ITERS)
    keep, gain = coefficients(ITERS)
    density[...] = keep * keep * density[...] + keep * gain * crossed + gain * gain * squared
    cur[...] = keep * cur[...] + gain * applied
    slab_rows = capacity // members
    slab[...] = cur[pl.ds(pl.multiple_of(member * slab_rows, slab_rows), slab_rows), :]
    for copy in sends:
        copy.wait_send()


def iterate(half, guess, left_env, right_env, block_rows, charges):
    capacity, width = guess.shape
    terms = left_env.shape[0]
    sectors = lax.axis_size("sec")
    members = lax.axis_size("mpo")
    tiles = half // width
    depths = capacity // width
    lent = max(capacity - half, 16)
    entries = MEAN * sectors * width
    dma = pltpu.SemaphoreType.DMA
    vmem = pl.BlockSpec(memory_space=pltpu.VMEM)
    smem = pl.BlockSpec(memory_space=pltpu.SMEM)
    hbm = pl.BlockSpec(memory_space=pl.ANY)
    return pl.pallas_call(
        functools.partial(iterate_kernel, sectors, members, entries, half),
        out_shape=(
            jax.ShapeDtypeStruct((capacity // members, width), jnp.float32),
            jax.ShapeDtypeStruct((width, width), jnp.float32),
        ),
        in_specs=[smem, smem, vmem, hbm, hbm],
        out_specs=(vmem, vmem),
        scratch_shapes=[
            pltpu.VMEM((terms, depths, capacity, width), left_env.dtype),
            pltpu.VMEM((terms, width, width), right_env.dtype),
            pltpu.VMEM((ITERS + 1, 6, half, width), jnp.bfloat16),
            pltpu.VMEM((capacity, width), jnp.float32),
            pltpu.VMEM((half // members, width), jnp.float32),
            pltpu.VMEM((capacity, width), jnp.float32),
            pltpu.VMEM((ITERS + 1, lent, width), jnp.bfloat16),
            pltpu.VMEM((ITERS + 1, lent, width), jnp.bfloat16),
            pltpu.VMEM((ITERS, half, width), jnp.bfloat16),
            pltpu.VMEM((ITERS, members, half // members, width), jnp.bfloat16),
            pltpu.VMEM((ITERS + 1, sectors, 8, 128), jnp.float32),
            dma((depths + 1,)),
            dma((ITERS + 1, members - 1, tiles)),
            dma((ITERS + 1, members, tiles)),
            dma((ITERS, members, tiles)),
            dma((ITERS, members, tiles)),
            dma((ITERS, members, tiles)),
            dma((ITERS, members, tiles)),
            dma((ITERS + 1, tiles)),
            dma((ITERS + 1, tiles)),
            dma((ITERS, 2, tiles)),
            dma((ITERS, 2, tiles)),
            dma((ITERS + 1,)),
            dma((ITERS + 1,)),
            dma((ITERS, members - 1, tiles)),
            dma((ITERS, members, tiles)),
            dma((ITERS + 1, sectors)),
            dma((ITERS + 1, sectors)),
        ],
        compiler_params=pltpu.CompilerParams(
            collective_id=0 if half < capacity else 1,
            has_side_effects=True, vmem_limit_bytes=56 * 1024 * 1024,
        ),
    )(block_rows, charges, guess, left_env, right_env)


small_residual = 3e-4


def exact_dot(left, right, dims):
    return lax.dot_general(
        left, right, (dims, ((), ())), precision=highest, preferred_element_type=jnp.float32
    )


def truncate_kernel(ranks, density, slab, copied, out, gram, pair):
    width = density.shape[0]
    copied[...] = slab[...]
    rows = lax.broadcasted_iota(jnp.int32, (width, width), 0)
    lanes = lax.broadcasted_iota(jnp.int32, (width, width), 1)
    identity = jnp.where(rows == lanes, 1.0, 0.0)
    full = identity + density[...] / MEAN
    kept = ranks[lax.axis_index("sec")]
    basis = jnp.where(lanes < kept, full, 0.0)
    basis_t = jnp.where(rows < kept, full, 0.0)
    matrix = exact_dot(basis_t, basis, ((1,), (0,))) + jnp.where(rows < kept, 0.0, identity)
    gram[...] = matrix
    largest = jnp.max(jnp.sum(jnp.abs(matrix), axis=0, keepdims=True))
    scale = 2.0 / (1.0 + largest)
    pair[:width, :] = identity - scale * matrix
    pair[width:, :] = scale * identity

    def unfinished(bound):
        return bound > small_residual

    def step(bound):
        square = bound * bound
        grow = 2.0 / (2.0 - square)
        product = exact_dot(pair[...], pair[:width, :], ((1,), (0,)))
        pair[width:, :] = grow * (pair[width:, :] + product[width:, :])
        pair[:width, :] = (1.0 - grow) * identity + grow * product[:width, :]
        return square / (2.0 - square)

    lax.while_loop(unfinished, step, (largest - 1.0) / (largest + 1.0))
    inverse = pair[width:, :]
    coords = exact_dot(slab[...], basis, ((1,), (0,)))
    solved = exact_dot(coords, inverse, ((1,), (0,)))
    rest = coords - exact_dot(solved, gram[...], ((1,), (0,)))
    solved = solved + exact_dot(rest, inverse, ((1,), (0,)))
    out[...] = exact_dot(solved, basis_t, ((1,), (0,)))


def truncate(density, slab, ranks):
    width = density.shape[0]
    vmem = pl.BlockSpec(memory_space=pltpu.VMEM)
    return pl.pallas_call(
        truncate_kernel,
        out_shape=(jax.ShapeDtypeStruct(slab.shape, jnp.float32),) * 2,
        in_specs=[pl.BlockSpec(memory_space=pltpu.SMEM), vmem, vmem],
        out_specs=(vmem, vmem),
        scratch_shapes=[
            pltpu.VMEM((width, width), jnp.float32),
            pltpu.VMEM((2 * width, width), jnp.float32),
        ],
    )(ranks, density, slab)


def shards(guess, left_env, right_env, block_rows, charges, ranks):
    capacity, width = guess.shape
    half = capacity - width
    shared = 2 * half - capacity
    ids = jnp.arange(block_rows.shape[0])
    pairs = ids[:, None] // 2 == ids[None, :] // 2
    clash = (block_rows[:, None] > half) & (block_rows[None, :] > shared) & pairs & (ids[:, None] != ids[None, :])
    fits = jnp.logical_not(jnp.any(clash))
    slab, density = lax.cond(
        fits, functools.partial(iterate, half), functools.partial(iterate, capacity),
        guess, left_env, right_env, block_rows, charges,
    )
    return truncate(density, slab, ranks)


def solution(mesh):
    return jax.shard_map(
        shards,
        mesh=mesh,
        in_specs=(P("sec", None), P("mpo", "sec", None), P("mpo", "sec", None), P(), P("mpo"), P()),
        out_specs=(P(("sec", "mpo"), None), P(("sec", "mpo"), None)),
        check_vma=False,
    )
```

```python
import functools

import jax
import jax.numpy as jnp
from jax import lax
from jax.experimental import pallas as pl
from jax.experimental.pallas import tpu as pltpu
from jax.sharding import PartitionSpec as P

MEAN = 256
ITERS = 4


epsilon = 1e-06
step_size = 0.1
highest = lax.Precision.HIGHEST


def row_sum(values):
    return jnp.sum(jnp.sum(values.reshape(-1, 8, 128), axis=0), axis=0, keepdims=True)


def arrival_order(member, members):
    steps = [(-1, 1), (1, -1)][member >= members // 2]
    order = [member]
    for d in range(1, members):
        order += [member + s * d for s in steps if 0 <= member + s * d < members]
    return order


def reduce_order(member, members):
    order = arrival_order(member, members)[1:]
    far = 1 if member < members // 2 else -1
    return sorted(order, key=lambda other: -(abs(other - member) * 2 + ((other - member) * far > 0)))


def transposed_dot(left, right):
    return lax.dot_general(left, right, (((0,), (0,)), ((), ())), preferred_element_type=jnp.float32)


def iterate_kernel(
    sectors, members, entries, half,
    block_rows, charges, guess, left_hbm, right_hbm, slab, density,
    left, right, xbuf, acc, app_chunk, cur, ex_out, ex_in, rs_out, rs_in, scal,
    load_sem, z_s, z_r, n_s, n_r, f_s, f_r, b_s, b_r, p_s, p_r, e_s, e_r, rs_s, rs_r, sc_s, sc_r,
):
    sector = lax.axis_index("sec")
    member = lax.axis_index("mpo")
    capacity, width = guess.shape
    packed = half < capacity
    shared = 2 * half - capacity
    tiles = -(-half // width)
    depths = left.shape[1]

    def deep(q):
        return min(width, half - q * width)

    def piece_rows(q):
        return deep(q) // members

    def part_of(q):
        return pl.ds(q * width // members, piece_rows(q))

    terms = left.shape[0]
    chips = sectors // 2
    parity = lax.rem(sector, 2)
    chip = sector // 2
    odd = lax.rem(chip, 2)
    sibling = sector + 1 - 2 * parity
    ahead = lax.rem(sector + 2, sectors)
    behind = lax.rem(sector + sectors - 2, sectors)
    square = chips == 4
    sends = []

    loads = [pltpu.make_async_copy(right_hbm, right, load_sem.at[depths])]
    for i in range(depths):
        loads.append(pltpu.make_async_copy(
            left_hbm.at[:, :, pl.ds(i * width, width)], left.at[:, i], load_sem.at[i]
        ))
    for load in loads:
        load.start()

    barrier = pltpu.get_barrier_semaphore()
    for d in range(1, sectors):
        pl.semaphore_signal(
            barrier, inc=1, device_id=(lax.rem(sector + d, sectors), member),
            device_id_type=pl.DeviceIdType.MESH,
        )
    for d in range(1, members):
        pl.semaphore_signal(
            barrier, inc=1, device_id=(sector, lax.rem(member + d, members)),
            device_id_type=pl.DeviceIdType.MESH,
        )
    pl.semaphore_wait(barrier, sectors + members - 2)

    def remote(src, dst, send, recv, sec, mpo):
        return pltpu.make_async_remote_copy(
            src_ref=src, dst_ref=dst, send_sem=send, recv_sem=recv,
            device_id=(sec, mpo), device_id_type=pl.DeviceIdType.MESH,
        )

    def launch(copy):
        copy.start()
        sends.append(copy)

    def sent():
        while sends:
            sends.pop().wait_send()

    def by_member(table):
        value = jnp.int32(table[0])
        for m in range(1, members):
            value = jnp.where(member == m, table[m], value)
        return value

    def tile_rows(q):
        return pl.ds(q * width, deep(q))

    def piece_of(j, q):
        return pl.ds(pl.multiple_of(q * width + j * piece_rows(q), piece_rows(q)), piece_rows(q))

    order = [by_member([arrival_order(m, members)[r] for m in range(members)]) for r in range(members)]
    targets = [by_member([reduce_order(m, members)[r] for m in range(members)]) for r in range(members - 1)]
    if square:
        near = jnp.where(odd == 1, behind, ahead)
        across = lax.rem(sector + sectors // 2, sectors)
        distant = jnp.where(odd == 1, ahead, behind)
        near_shift = jnp.where(odd == 1, 2, -2)
        fifth_far = parity == odd
    else:
        near, distant = behind, ahead
        near_shift = jnp.int32(-2)
        fifth_far = parity == 0
    far_shift = -near_shift

    def z_copy(k, t, q):
        rows = piece_of(member, q)
        return remote(
            xbuf.at[k, 0, rows], xbuf.at[k, 0, rows], z_s.at[k, t, q], z_r.at[k, member, q],
            sector, targets[t],
        )

    def z_wait(k, j, q):
        arrived(k, 0, piece_of(j, q), z_s.at[k, 0, q], z_r.at[k, j, q])

    def near_copy(k, j, q):
        rows = piece_of(j, q)
        return remote(
            xbuf.at[k, 0, rows], xbuf.at[k, 2, rows], n_s.at[k, j, q], n_r.at[k, j, q], near, member,
        )

    def far_copy(k, j, q):
        rows = piece_of(j, q)
        return remote(
            xbuf.at[k, 0, rows], xbuf.at[k, 3, rows], f_s.at[k, j, q], f_r.at[k, j, q], distant, member,
        )

    def far_relay(k, j, q):
        rows = piece_of(j, q)
        launch(remote(
            xbuf.at[k, 2, rows], xbuf.at[k, 3, rows], f_s.at[k, j, q], f_r.at[k, j, q], across, member,
        ))

    def sibling_send(k, q):
        rows = tile_rows(q)
        launch(remote(
            xbuf.at[k, 0, rows], xbuf.at[k, 1, rows], b_s.at[k, q], b_r.at[k, q], sibling, member,
        ))

    def pass_send(k, q, far):
        rows = tile_rows(q)
        launch(remote(
            xbuf.at[k, 2 + far, rows], xbuf.at[k, 4 + far, rows],
            p_s.at[k, far, q], p_r.at[k, far, q], sibling, member,
        ))

    def exchange(k):
        return remote(ex_out.at[k], ex_in.at[k], e_s.at[k], e_r.at[k], sibling, member)

    def arrived(k, slot, rows, send, recv):
        remote(xbuf.at[k, slot, rows], xbuf.at[k, slot, rows], send, recv, sibling, member).wait_recv()

    def rs_copy(k, t, q):
        return remote(
            rs_out.at[k, piece_of(targets[t], q)], rs_in.at[k, member, part_of(q)],
            rs_s.at[k, t, q], rs_r.at[k, member, q], sector, targets[t],
        )

    def scal_copy(k, d):
        return remote(
            scal.at[k, sector], scal.at[k, sector],
            sc_s.at[k, d - 1], sc_r.at[k, d - 1], lax.rem(sector + d, sectors), member,
        )

    def scal_wait(k):
        for d in range(1, sectors):
            src = lax.rem(sector - d + sectors, sectors)
            remote(
                scal.at[k, src], scal.at[k, src],
                sc_s.at[k, d - 1], sc_r.at[k, d - 1], src, member,
            ).wait_recv()

    def term_of(charge):
        index = jnp.int32(0)
        for i in range(1, terms):
            index = jnp.where(charges[i] == charge, i, index)
        return index

    def count_of(shift):
        return block_rows[lax.rem(sector + shift + sectors, sectors)]

    own_rows, sibling_rows = count_of(0), block_rows[sibling]
    fifth = 2 * parity - 1
    both_far = jnp.where(fifth_far, 1, 0)
    term_own, term_sibling = term_of(0), term_of(2 * parity - 1)
    term_near, term_far, term_fifth = term_of(near_shift), term_of(far_shift), term_of(-fifth)

    def over(rows):
        return jnp.where(rows > half, 1, 0)

    mates = 1 - 2 * parity
    fifth_slot = 4 + both_far
    far_rows, near_rows = count_of(-far_shift), count_of(-near_shift)
    near_tail = over(count_of(-near_shift + mates))
    far_tail = over(count_of(-far_shift + mates))
    tasks = {
        0: (0, term_own, term_sibling, over(sibling_rows), 1),
        1: (1, term_sibling, term_own, over(own_rows), 1),
        2: (2, term_near, term_fifth, near_tail, 1 - both_far),
        3: (3, term_far, term_fifth, far_tail, both_far),
        4: (fifth_slot, term_fifth, term_fifth, 0, 1),
    }
    ends = (
        (term_near, over(near_rows), 1 - both_far), (term_far, over(far_rows), both_far),
    )

    def mix(k, slot, q, index, keep_rows=None):
        value = xbuf[k, slot, tile_rows(q), :]
        if keep_rows is not None:
            value = jnp.where(keep_rows > 0, value, jnp.zeros_like(value))
        return jnp.dot(value, right[index], preferred_element_type=jnp.float32).astype(jnp.bfloat16)

    def tile_task(k, group, q):
        slot, index, mate, tail, counted = tasks[group]
        keep_rows = None
        if not packed or q * width < shared or group == 4:
            tail = None
        else:
            index = jnp.where(tail > 0, mate, index)
            keep_rows = 1 - tail * (1 - counted)
        return index, q, tail, mix(k, slot, q, index, keep_rows)

    def passed_task(k, q, far):
        index, tail, counted = ends[far]
        index = jnp.where(tail > 0, index, term_fifth)
        return index, q, tail, mix(k, 4 + far, q, index, jnp.maximum(tail, counted))

    def add(task, rows=pl.ds(0, capacity), first=False):
        index, q, tail, mixed = task
        column = half + q * width - shared
        if tail is None:
            factor = left[index, q, rows, pl.ds(0, deep(q))]
        elif column % width == 0:
            factor = left[index, jnp.where(tail > 0, column // width, q), rows, pl.ds(0, deep(q))]
        else:
            factor = jnp.where(
                tail > 0, left[index, column // width, rows, pl.ds(column % width, deep(q))],
                left[index, q, rows, pl.ds(0, deep(q))],
            )
        value = jnp.dot(factor, mixed, preferred_element_type=jnp.float32)
        acc[rows, :] = value if first else acc[rows, :] + value

    def block(k):
        if not packed:
            return xbuf[k, 0].astype(jnp.float32)
        ending = xbuf[k, 0, pl.ds(shared, half - shared), :]
        beyond = xbuf[k, 1, pl.ds(shared, half - shared), :]
        return jnp.concatenate([
            xbuf[k, 0, pl.ds(0, shared), :],
            jnp.where(sibling_rows > half, jnp.zeros_like(ending), ending),
            jnp.where(own_rows > half, beyond, jnp.zeros_like(beyond)),
        ], axis=0).astype(jnp.float32)

    def send_sums(k, first, second, third):
        rows = [row_sum(first), row_sum(second), row_sum(third), jnp.zeros((5, 128), jnp.float32)]
        scal[k, sector] = jnp.concatenate(rows, axis=0)
        for d in range(1, sectors):
            launch(scal_copy(k, d))

    def coefficients(k, opening=False):
        sums = jnp.sum(jnp.sum(scal[k], axis=0), axis=1, keepdims=True)
        self_dot, cross_dot, image_dot = sums[0:1], sums[1:2], sums[2:3]
        if opening:
            scale = lax.rsqrt(self_dot / entries + epsilon)
            return scale, scale
        rayleigh = cross_dot / (self_dot + epsilon)
        squares = self_dot * (1.0 - (step_size * rayleigh) ** 2) + step_size**2 * image_dot
        scale = lax.rsqrt(squares / entries + epsilon)
        return (1.0 + step_size * rayleigh) * scale, -step_size * scale

    def state_sums(k, keep, gain):
        state = keep * cur[...] + jnp.where(k == 1, 0.0, gain) * block(k - 1)
        cur[...] = state
        applied = block(k)
        send_sums(k, state * state, state * applied, applied * applied)

    def pack(k, q, rows):
        if not packed or q * width < shared:
            return rows
        if q * width == shared:
            exchange(k).wait_recv()
        return jnp.where(sibling_rows > half, ex_in[k, pl.ds(q * width - shared, deep(q)), :], rows)

    def offer(k, rows):
        ex_out[k] = rows.astype(jnp.bfloat16)
        launch(exchange(k))

    positions = lax.broadcasted_iota(jnp.int32, (capacity, width), 0)
    start = jnp.where(positions < own_rows, guess[...], 0.0)
    cur[...] = start
    if packed:
        offer(ITERS, cur[pl.ds(half, capacity - half), :])
    for q in range(tiles):
        xbuf[0, 0, tile_rows(q)] = pack(ITERS, q, cur[tile_rows(q), :].astype(jnp.bfloat16))
        for j in range(members):
            launch(near_copy(0, j, q))
            if not square:
                launch(far_copy(0, j, q))
        sibling_send(0, q)

    def near_tile(k, q, opening=False):
        for j in order:
            arrived(k, 2, piece_of(j, q), n_s.at[k, j, q], n_r.at[k, j, q])
            if opening and square:
                far_relay(k, j, q)
        pass_send(k, q, 0)

    def far_tile(k, q):
        for j in order:
            arrived(k, 3, piece_of(j, q), f_s.at[k, j, q], f_r.at[k, j, q])
        pass_send(k, q, 1)

    def sibling_tile(k, q):
        arrived(k, 1, tile_rows(q), b_s.at[k, q], b_r.at[k, q])

    def passed_tile(k, q, far):
        arrived(k, 4 + far, tile_rows(q), p_s.at[k, far, q], p_r.at[k, far, q])

    def gather(k, final=False):
        for q in range(tiles):
            for j in order[1:]:
                z_wait(k, j, q)
                if not final:
                    launch(far_copy(k, j, q))
                    launch(near_copy(k, j, q))
            sibling_send(k, q)
            if not final:
                add(tile_task(k, 0, q), first=q == 0)

    def iteration(k, keep, gain, opening=False):
        if opening:
            for q in range(tiles):
                add(tile_task(k, 0, q), first=q == 0)
        else:
            gather(k)
        for q in range(tiles):
            if not opening:
                near_tile(k, q)
            elif q == 0:
                for p in range(tiles):
                    near_tile(k, p, opening)
            add(tile_task(k, 2, q))
            far_tile(k, q)
            if q == tiles - 1:
                passed_tile(k, q, 0)
                if packed:
                    add(passed_task(k, q, 0))
            add(tile_task(k, 3, q))
            if q == 0:
                for i in range(tiles):
                    sibling_tile(k, i)
                    add(tile_task(k, 1, i))
            if q < tiles - 1:
                passed_tile(k, q, 0)
                passed_tile(k, q, 1)
                if packed and q * width >= shared:
                    add(passed_task(k, q, 0))
                    add(passed_task(k, q, 1))
                else:
                    add(tile_task(k, 4, q))
        passed_tile(k, tiles - 1, 1)
        if packed:
            last = passed_task(k, tiles - 1, 1)
            rows = pl.ds(half, capacity - half)
            add(last, rows)
            offer(k, acc[rows, :])
        else:
            last = tile_task(k, 4, tiles - 1)
        earlier = list(sends)
        sends.clear()
        for q in range(tiles):
            add(last, tile_rows(q))
            rs_out[k, tile_rows(q)] = pack(k, q, acc[tile_rows(q), :].astype(jnp.bfloat16))
            for t in range(members - 1):
                launch(rs_copy(k, t, q))
        if opening:
            nothing = jnp.zeros((8, 128))
            send_sums(0, cur[...] * cur[...], nothing, nothing)
        else:
            state_sums(k, keep, gain)
        for copy in earlier:
            copy.wait_send()
        scal_wait(k)
        keep, gain = coefficients(k, opening)
        if not opening:
            for q in range(tiles):
                for t in range(members - 1):
                    z_copy(k, t, q).wait_send()
                far_copy(k, member, q).wait_send()
                near_copy(k, member, q).wait_send()
        for q in range(tiles):
            part, piece = part_of(q), piece_rows(q)
            mine = piece_of(member, q)
            image = acc[mine, :]
            first, limit = member * piece + q * width, own_rows
            if packed and q * width >= shared:
                borrowed = sibling_rows > half
                lent = pl.ds(pl.multiple_of(q * width - shared + member * piece, piece), piece)
                image = jnp.where(borrowed, ex_in[k, lent, :].astype(jnp.float32), image)
                first = jnp.where(borrowed, first - shared + half, first)
                limit = jnp.where(borrowed, sibling_rows, limit)
            for j in order[1:]:
                remote(
                    rs_in.at[k, j, part], rs_in.at[k, j, part],
                    rs_s.at[k, 0, q], rs_r.at[k, j, q], sibling, member,
                ).wait_recv()
                image = image + rs_in[k, j, part].astype(jnp.float32)
            positions = lax.broadcasted_iota(jnp.int32, (piece, width), 0) + first
            image = jnp.where(positions < limit, image, 0.0) * gain
            if not opening:
                image = image + keep * app_chunk[part, :]
            app_chunk[part, :] = image
            xbuf[k + 1, 0, mine] = image.astype(jnp.bfloat16)
            for t in reversed(range(members - 1)):
                z_copy(k + 1, t, q).start()
            copies = far_copy(k + 1, member, q), near_copy(k + 1, member, q)
            for copy in copies:
                if opening:
                    copy.start()
                else:
                    pl.when(k < ITERS - 1)(copy.start)
        sent()
        return keep, gain

    for load in loads:
        load.wait()
    keep, gain = iteration(0, None, None, opening=True)
    keep, gain = lax.fori_loop(1, ITERS, lambda k, pair: iteration(k, *pair), (keep, gain))

    state = keep * cur[...] + gain * block(ITERS - 1)
    cur[...] = state
    high = state.astype(jnp.bfloat16)
    low = (state - high.astype(jnp.float32)).astype(jnp.bfloat16)
    mixed = transposed_dot(high, low)
    density[...] = transposed_dot(high, high) + (mixed + mixed.T)
    gather(ITERS, final=True)
    for q in range(tiles):
        sibling_tile(ITERS, q)
    applied = block(ITERS)
    send_sums(ITERS, state * state, state * applied, applied * applied)
    final_step = applied.astype(jnp.bfloat16)
    crossed = transposed_dot(high, final_step) + transposed_dot(low, final_step)
    crossed = crossed + crossed.T
    squared = transposed_dot(final_step, final_step)
    scal_wait(ITERS)
    keep, gain = coefficients(ITERS)
    density[...] = keep * keep * density[...] + keep * gain * crossed + gain * gain * squared
    cur[...] = keep * cur[...] + gain * applied
    slab_rows = capacity // members
    slab[...] = cur[pl.ds(pl.multiple_of(member * slab_rows, slab_rows), slab_rows), :]
    sent()
    for q in range(tiles):
        for t in range(members - 1):
            z_copy(ITERS, t, q).wait_send()


def iterate(half, guess, left_env, right_env, block_rows, charges):
    capacity, width = guess.shape
    terms = left_env.shape[0]
    sectors = lax.axis_size("sec")
    members = lax.axis_size("mpo")
    tiles = -(-half // width)
    depths = capacity // width
    lent = max(capacity - half, 16)
    entries = MEAN * sectors * width
    dma = pltpu.SemaphoreType.DMA
    vmem = pl.BlockSpec(memory_space=pltpu.VMEM)
    smem = pl.BlockSpec(memory_space=pltpu.SMEM)
    hbm = pl.BlockSpec(memory_space=pl.ANY)
    return pl.pallas_call(
        functools.partial(iterate_kernel, sectors, members, entries, half),
        out_shape=(
            jax.ShapeDtypeStruct((capacity // members, width), jnp.float32),
            jax.ShapeDtypeStruct((width, width), jnp.float32),
        ),
        in_specs=[smem, smem, vmem, hbm, hbm],
        out_specs=(vmem, vmem),
        scratch_shapes=[
            pltpu.VMEM((terms, depths, capacity, width), left_env.dtype),
            pltpu.VMEM((terms, width, width), right_env.dtype),
            pltpu.VMEM((ITERS + 1, 6, half, width), jnp.bfloat16),
            pltpu.VMEM((capacity, width), jnp.float32),
            pltpu.VMEM((half // members, width), jnp.float32),
            pltpu.VMEM((capacity, width), jnp.float32),
            pltpu.VMEM((ITERS + 1, lent, width), jnp.bfloat16),
            pltpu.VMEM((ITERS + 1, lent, width), jnp.bfloat16),
            pltpu.VMEM((ITERS, half, width), jnp.bfloat16),
            pltpu.VMEM((ITERS, members, half // members, width), jnp.bfloat16),
            pltpu.VMEM((ITERS + 1, sectors, 8, 128), jnp.float32),
            dma((depths + 1,)),
            dma((ITERS + 1, members - 1, tiles)),
            dma((ITERS + 1, members, tiles)),
            dma((ITERS + 1, members, tiles)),
            dma((ITERS + 1, members, tiles)),
            dma((ITERS + 1, members, tiles)),
            dma((ITERS + 1, members, tiles)),
            dma((ITERS + 1, tiles)),
            dma((ITERS + 1, tiles)),
            dma((ITERS, 2, tiles)),
            dma((ITERS, 2, tiles)),
            dma((ITERS + 1,)),
            dma((ITERS + 1,)),
            dma((ITERS, members - 1, tiles)),
            dma((ITERS, members, tiles)),
            dma((ITERS + 1, sectors)),
            dma((ITERS + 1, sectors)),
        ],
        compiler_params=pltpu.CompilerParams(
            collective_id=(capacity - half) // (width // 2),
            has_side_effects=True, vmem_limit_bytes=56 * 1024 * 1024,
        ),
    )(block_rows, charges, guess, left_env, right_env)


small_residual = 3e-4


def exact_dot(left, right, dims):
    return lax.dot_general(
        left, right, (dims, ((), ())), precision=highest, preferred_element_type=jnp.float32
    )


def truncate_kernel(ranks, density, slab, copied, out, gram, pair):
    width = density.shape[0]
    copied[...] = slab[...]
    rows = lax.broadcasted_iota(jnp.int32, (width, width), 0)
    lanes = lax.broadcasted_iota(jnp.int32, (width, width), 1)
    identity = jnp.where(rows == lanes, 1.0, 0.0)
    full = identity + density[...] / MEAN
    kept = ranks[lax.axis_index("sec")]
    basis = jnp.where(lanes < kept, full, 0.0)
    basis_t = jnp.where(rows < kept, full, 0.0)
    matrix = exact_dot(basis_t, basis, ((1,), (0,))) + jnp.where(rows < kept, 0.0, identity)
    gram[...] = matrix
    largest = jnp.max(jnp.sum(jnp.abs(matrix), axis=0, keepdims=True))
    scale = 2.0 / (1.0 + largest)
    pair[:width, :] = identity - scale * matrix
    pair[width:, :] = scale * identity

    def unfinished(bound):
        return bound > small_residual

    def step(bound):
        square = bound * bound
        grow = 2.0 / (2.0 - square)
        product = exact_dot(pair[...], pair[:width, :], ((1,), (0,)))
        pair[width:, :] = grow * (pair[width:, :] + product[width:, :])
        pair[:width, :] = (1.0 - grow) * identity + grow * product[:width, :]
        return square / (2.0 - square)

    lax.while_loop(unfinished, step, (largest - 1.0) / (largest + 1.0))
    inverse = pair[width:, :]
    coords = exact_dot(slab[...], basis, ((1,), (0,)))
    solved = exact_dot(coords, inverse, ((1,), (0,)))
    rest = coords - exact_dot(solved, gram[...], ((1,), (0,)))
    solved = solved + exact_dot(rest, inverse, ((1,), (0,)))
    out[...] = exact_dot(solved, basis_t, ((1,), (0,)))


def truncate(density, slab, ranks):
    width = density.shape[0]
    vmem = pl.BlockSpec(memory_space=pltpu.VMEM)
    return pl.pallas_call(
        truncate_kernel,
        out_shape=(jax.ShapeDtypeStruct(slab.shape, jnp.float32),) * 2,
        in_specs=[pl.BlockSpec(memory_space=pltpu.SMEM), vmem, vmem],
        out_specs=(vmem, vmem),
        scratch_shapes=[
            pltpu.VMEM((width, width), jnp.float32),
            pltpu.VMEM((2 * width, width), jnp.float32),
        ],
    )(ranks, density, slab)


def shards(guess, left_env, right_env, block_rows, charges, ranks):
    capacity, width = guess.shape
    ids = jnp.arange(block_rows.shape[0])
    pairs = (ids[:, None] // 2 == ids[None, :] // 2) & (ids[:, None] != ids[None, :])
    most, least = block_rows[:, None], block_rows[None, :]
    halves = [capacity - width, capacity - width // 2, capacity]
    needs = sum(
        ((most > half) & (least > 2 * half - capacity) & pairs).astype(jnp.int32) for half in halves[:-1]
    )
    choice = jnp.max(needs)
    slab, density = lax.switch(
        choice, [functools.partial(iterate, half) for half in halves],
        guess, left_env, right_env, block_rows, charges,
    )
    return truncate(density, slab, ranks)


def solution(mesh):
    return jax.shard_map(
        shards,
        mesh=mesh,
        in_specs=(P("sec", None), P("mpo", "sec", None), P("mpo", "sec", None), P(), P("mpo"), P()),
        out_specs=(P(("sec", "mpo"), None), P(("sec", "mpo"), None)),
        check_vma=False,
    )
```

```python
import functools

import jax
import jax.numpy as jnp
from jax import lax
from jax.experimental import pallas as pl
from jax.experimental.pallas import tpu as pltpu
from jax.sharding import PartitionSpec as P

MEAN = 256
ITERS = 4


epsilon = 1e-06
step_size = 0.1
highest = lax.Precision.HIGHEST


def row_sum(values):
    return jnp.sum(jnp.sum(values.reshape(-1, 8, 128), axis=0), axis=0, keepdims=True)


def arrival_order(member, members):
    steps = [(-1, 1), (1, -1)][member >= members // 2]
    order = [member]
    for d in range(1, members):
        order += [member + s * d for s in steps if 0 <= member + s * d < members]
    return order


def transposed_dot(left, right):
    return lax.dot_general(left, right, (((0,), (0,)), ((), ())), preferred_element_type=jnp.float32)


def iterate_kernel(
    sectors, members, entries, half,
    block_rows, charges, guess, left_hbm, right_hbm, slab, density,
    left, right, xbuf, acc, app_chunk, cur, ex_out, ex_in, rs_out, rs_in, scal,
    load_sem, z_s, z_r, n_s, n_r, f_s, f_r, b_s, b_r, p_s, p_r, e_s, e_r, rs_s, rs_r, sc_s, sc_r,
):
    sector = lax.axis_index("sec")
    member = lax.axis_index("mpo")
    capacity, width = guess.shape
    packed = half < capacity
    shared = 2 * half - capacity
    tiles = -(-half // width)
    depths = left.shape[1]

    def deep(q):
        return min(width, half - q * width)

    def piece_rows(q):
        return deep(q) // members

    def part_of(q):
        return pl.ds(q * width // members, piece_rows(q))

    terms = left.shape[0]
    chips = sectors // 2
    parity = lax.rem(sector, 2)
    chip = sector // 2
    odd = lax.rem(chip, 2)
    sibling = sector + 1 - 2 * parity
    ahead = lax.rem(sector + 2, sectors)
    behind = lax.rem(sector + sectors - 2, sectors)
    square = chips == 4
    sends = []

    loads = [pltpu.make_async_copy(right_hbm, right, load_sem.at[depths])]
    for i in range(depths):
        loads.append(pltpu.make_async_copy(
            left_hbm.at[:, :, pl.ds(i * width, width)], left.at[:, i], load_sem.at[i]
        ))
    for load in loads:
        load.start()

    barrier = pltpu.get_barrier_semaphore()
    for d in range(1, sectors):
        pl.semaphore_signal(
            barrier, inc=1, device_id=(lax.rem(sector + d, sectors), member),
            device_id_type=pl.DeviceIdType.MESH,
        )
    for d in range(1, members):
        pl.semaphore_signal(
            barrier, inc=1, device_id=(sector, lax.rem(member + d, members)),
            device_id_type=pl.DeviceIdType.MESH,
        )
    pl.semaphore_wait(barrier, sectors + members - 2)

    def remote(src, dst, send, recv, sec, mpo):
        return pltpu.make_async_remote_copy(
            src_ref=src, dst_ref=dst, send_sem=send, recv_sem=recv,
            device_id=(sec, mpo), device_id_type=pl.DeviceIdType.MESH,
        )

    def launch(copy):
        copy.start()
        sends.append(copy)

    def sent():
        while sends:
            sends.pop().wait_send()

    def by_member(table):
        value = jnp.int32(table[0])
        for m in range(1, members):
            value = jnp.where(member == m, table[m], value)
        return value

    def tile_rows(q):
        return pl.ds(q * width, deep(q))

    def piece_of(j, q):
        return pl.ds(pl.multiple_of(q * width + j * piece_rows(q), piece_rows(q)), piece_rows(q))

    order = [by_member([arrival_order(m, members)[r] for m in range(members)]) for r in range(members)]
    targets = order[1:]
    if square:
        near = jnp.where(odd == 1, behind, ahead)
        across = lax.rem(sector + sectors // 2, sectors)
        distant = jnp.where(odd == 1, ahead, behind)
        near_shift = jnp.where(odd == 1, 2, -2)
        fifth_far = parity == odd
    else:
        near, distant = behind, ahead
        near_shift = jnp.int32(-2)
        fifth_far = parity == 0
    far_shift = -near_shift

    def z_copy(k, t, q):
        rows = piece_of(member, q)
        return remote(
            xbuf.at[k, 0, rows], xbuf.at[k, 0, rows], z_s.at[k, t, q], z_r.at[k, member, q],
            sector, targets[t],
        )

    def z_wait(k, j, q):
        arrived(k, 0, piece_of(j, q), z_s.at[k, 0, q], z_r.at[k, j, q])

    def near_copy(k, j, q):
        rows = piece_of(j, q)
        return remote(
            xbuf.at[k, 0, rows], xbuf.at[k, 2, rows], n_s.at[k, j, q], n_r.at[k, j, q], near, member,
        )

    def far_copy(k, j, q):
        rows = piece_of(j, q)
        return remote(
            xbuf.at[k, 0, rows], xbuf.at[k, 3, rows], f_s.at[k, j, q], f_r.at[k, j, q], distant, member,
        )

    def far_relay(k, j, q):
        rows = piece_of(j, q)
        launch(remote(
            xbuf.at[k, 2, rows], xbuf.at[k, 3, rows], f_s.at[k, j, q], f_r.at[k, j, q], across, member,
        ))

    def sibling_send(k, q):
        rows = tile_rows(q)
        launch(remote(
            xbuf.at[k, 0, rows], xbuf.at[k, 1, rows], b_s.at[k, q], b_r.at[k, q], sibling, member,
        ))

    def pass_send(k, q, far):
        rows = tile_rows(q)
        launch(remote(
            xbuf.at[k, 2 + far, rows], xbuf.at[k, 4 + far, rows],
            p_s.at[k, far, q], p_r.at[k, far, q], sibling, member,
        ))

    def exchange(k):
        return remote(ex_out.at[k], ex_in.at[k], e_s.at[k], e_r.at[k], sibling, member)

    def arrived(k, slot, rows, send, recv):
        remote(xbuf.at[k, slot, rows], xbuf.at[k, slot, rows], send, recv, sibling, member).wait_recv()

    def rs_copy(k, t, q):
        return remote(
            rs_out.at[k, piece_of(targets[t], q)], rs_in.at[k, member, part_of(q)],
            rs_s.at[k, t, q], rs_r.at[k, member, q], sector, targets[t],
        )

    def scal_copy(k, d):
        return remote(
            scal.at[k, sector], scal.at[k, sector],
            sc_s.at[k, d - 1], sc_r.at[k, d - 1], lax.rem(sector + d, sectors), member,
        )

    def scal_wait(k):
        for d in range(1, sectors):
            src = lax.rem(sector - d + sectors, sectors)
            remote(
                scal.at[k, src], scal.at[k, src],
                sc_s.at[k, d - 1], sc_r.at[k, d - 1], src, member,
            ).wait_recv()

    def term_of(charge):
        index = jnp.int32(0)
        for i in range(1, terms):
            index = jnp.where(charges[i] == charge, i, index)
        return index

    def count_of(shift):
        return block_rows[lax.rem(sector + shift + sectors, sectors)]

    own_rows, sibling_rows = count_of(0), block_rows[sibling]
    fifth = 2 * parity - 1
    both_far = jnp.where(fifth_far, 1, 0)
    term_own, term_sibling = term_of(0), term_of(2 * parity - 1)
    term_near, term_far, term_fifth = term_of(near_shift), term_of(far_shift), term_of(-fifth)

    def over(rows):
        return jnp.where(rows > half, 1, 0)

    mates = 1 - 2 * parity
    fifth_slot = 4 + both_far
    far_rows, near_rows = count_of(-far_shift), count_of(-near_shift)
    near_tail = over(count_of(-near_shift + mates))
    far_tail = over(count_of(-far_shift + mates))
    tasks = {
        0: (0, term_own, term_sibling, over(sibling_rows), 1),
        1: (1, term_sibling, term_own, over(own_rows), 1),
        2: (2, term_near, term_fifth, near_tail, 1 - both_far),
        3: (3, term_far, term_fifth, far_tail, both_far),
        4: (fifth_slot, term_fifth, term_fifth, 0, 1),
    }
    ends = (
        (term_near, over(near_rows), 1 - both_far), (term_far, over(far_rows), both_far),
    )

    def mix(k, slot, q, index, keep_rows=None):
        value = xbuf[k, slot, tile_rows(q), :]
        if keep_rows is not None:
            value = jnp.where(keep_rows > 0, value, jnp.zeros_like(value))
        return jnp.dot(value, right[index], preferred_element_type=jnp.float32).astype(jnp.bfloat16)

    def tile_task(k, group, q):
        slot, index, mate, tail, counted = tasks[group]
        keep_rows = None
        if not packed or q * width < shared or group == 4:
            tail = None
        else:
            index = jnp.where(tail > 0, mate, index)
            keep_rows = 1 - tail * (1 - counted)
        return index, q, tail, mix(k, slot, q, index, keep_rows)

    def passed_task(k, q, far):
        index, tail, counted = ends[far]
        index = jnp.where(tail > 0, index, term_fifth)
        return index, q, tail, mix(k, 4 + far, q, index, jnp.maximum(tail, counted))

    def add(task, rows=pl.ds(0, capacity), first=False):
        index, q, tail, mixed = task
        column = half + q * width - shared
        if tail is None:
            factor = left[index, q, rows, pl.ds(0, deep(q))]
        elif column % width == 0:
            factor = left[index, jnp.where(tail > 0, column // width, q), rows, pl.ds(0, deep(q))]
        else:
            factor = jnp.where(
                tail > 0, left[index, column // width, rows, pl.ds(column % width, deep(q))],
                left[index, q, rows, pl.ds(0, deep(q))],
            )
        value = jnp.dot(factor, mixed, preferred_element_type=jnp.float32)
        acc[rows, :] = value if first else acc[rows, :] + value

    def block(k):
        if not packed:
            return xbuf[k, 0].astype(jnp.float32)
        ending = xbuf[k, 0, pl.ds(shared, half - shared), :]
        beyond = xbuf[k, 1, pl.ds(shared, half - shared), :]
        return jnp.concatenate([
            xbuf[k, 0, pl.ds(0, shared), :],
            jnp.where(sibling_rows > half, jnp.zeros_like(ending), ending),
            jnp.where(own_rows > half, beyond, jnp.zeros_like(beyond)),
        ], axis=0).astype(jnp.float32)

    def send_sums(k, first, second, third):
        rows = [row_sum(first), row_sum(second), row_sum(third), jnp.zeros((5, 128), jnp.float32)]
        scal[k, sector] = jnp.concatenate(rows, axis=0)
        for d in range(1, sectors):
            launch(scal_copy(k, d))

    def coefficients(k, opening=False):
        sums = jnp.sum(jnp.sum(scal[k], axis=0), axis=1, keepdims=True)
        self_dot, cross_dot, image_dot = sums[0:1], sums[1:2], sums[2:3]
        if opening:
            scale = lax.rsqrt(self_dot / entries + epsilon)
            return scale, scale
        rayleigh = cross_dot / (self_dot + epsilon)
        squares = self_dot * (1.0 - (step_size * rayleigh) ** 2) + step_size**2 * image_dot
        scale = lax.rsqrt(squares / entries + epsilon)
        return (1.0 + step_size * rayleigh) * scale, -step_size * scale

    def state_sums(k, keep, gain):
        state = keep * cur[...] + jnp.where(k == 1, 0.0, gain) * block(k - 1)
        cur[...] = state
        applied = block(k)
        send_sums(k, state * state, state * applied, applied * applied)

    def pack(k, q, rows):
        if not packed or q * width < shared:
            return rows
        if q * width == shared:
            exchange(k).wait_recv()
        return jnp.where(sibling_rows > half, ex_in[k, pl.ds(q * width - shared, deep(q)), :], rows)

    def offer(k, rows):
        ex_out[k] = rows.astype(jnp.bfloat16)
        launch(exchange(k))

    positions = lax.broadcasted_iota(jnp.int32, (capacity, width), 0)
    start = jnp.where(positions < own_rows, guess[...], 0.0)
    cur[...] = start
    if packed:
        offer(ITERS, cur[pl.ds(half, capacity - half), :])
    for q in range(tiles):
        xbuf[0, 0, tile_rows(q)] = pack(ITERS, q, cur[tile_rows(q), :].astype(jnp.bfloat16))
        for j in range(members):
            launch(near_copy(0, j, q))
            if not square:
                launch(far_copy(0, j, q))
        sibling_send(0, q)

    def near_tile(k, q, opening=False):
        for j in order:
            arrived(k, 2, piece_of(j, q), n_s.at[k, j, q], n_r.at[k, j, q])
            if opening and square:
                far_relay(k, j, q)
        pass_send(k, q, 0)

    def far_tile(k, q):
        for j in order:
            arrived(k, 3, piece_of(j, q), f_s.at[k, j, q], f_r.at[k, j, q])
        pass_send(k, q, 1)

    def sibling_tile(k, q):
        arrived(k, 1, tile_rows(q), b_s.at[k, q], b_r.at[k, q])

    def passed_tile(k, q, far):
        arrived(k, 4 + far, tile_rows(q), p_s.at[k, far, q], p_r.at[k, far, q])

    def gather(k, final=False):
        for q in range(tiles):
            for j in order[1:]:
                z_wait(k, j, q)
                if not final:
                    launch(far_copy(k, j, q))
                    launch(near_copy(k, j, q))
            sibling_send(k, q)
            if not final:
                add(tile_task(k, 0, q), first=q == 0)

    def iteration(k, keep, gain, opening=False):
        if opening:
            for q in range(tiles):
                add(tile_task(k, 0, q), first=q == 0)
        else:
            gather(k)
        for q in range(tiles):
            if not opening:
                near_tile(k, q)
            elif q == 0:
                for p in range(tiles):
                    near_tile(k, p, opening)
            add(tile_task(k, 2, q))
            far_tile(k, q)
            if q == tiles - 1:
                passed_tile(k, q, 0)
                if packed:
                    add(passed_task(k, q, 0))
            add(tile_task(k, 3, q))
            if q == 0:
                for i in range(tiles):
                    sibling_tile(k, i)
                    add(tile_task(k, 1, i))
            if q < tiles - 1:
                passed_tile(k, q, 0)
                passed_tile(k, q, 1)
                if packed and q * width >= shared:
                    add(passed_task(k, q, 0))
                    add(passed_task(k, q, 1))
                else:
                    add(tile_task(k, 4, q))
        passed_tile(k, tiles - 1, 1)
        if packed:
            last = passed_task(k, tiles - 1, 1)
            rows = pl.ds(half, capacity - half)
            add(last, rows)
            offer(k, acc[rows, :])
        else:
            last = tile_task(k, 4, tiles - 1)
        earlier = list(sends)
        sends.clear()
        for q in range(tiles):
            add(last, tile_rows(q))
            rs_out[k, tile_rows(q)] = pack(k, q, acc[tile_rows(q), :].astype(jnp.bfloat16))
            for t in range(members - 1):
                launch(rs_copy(k, t, q))
        if opening:
            nothing = jnp.zeros((8, 128))
            send_sums(0, cur[...] * cur[...], nothing, nothing)
        else:
            state_sums(k, keep, gain)
        for copy in earlier:
            copy.wait_send()
        scal_wait(k)
        keep, gain = coefficients(k, opening)
        if not opening:
            for q in range(tiles):
                for t in range(members - 1):
                    z_copy(k, t, q).wait_send()
                far_copy(k, member, q).wait_send()
                near_copy(k, member, q).wait_send()
        for q in range(tiles):
            part, piece = part_of(q), piece_rows(q)
            mine = piece_of(member, q)
            image = acc[mine, :]
            first, limit = member * piece + q * width, own_rows
            if packed and q * width >= shared:
                borrowed = sibling_rows > half
                lent = pl.ds(pl.multiple_of(q * width - shared + member * piece, piece), piece)
                image = jnp.where(borrowed, ex_in[k, lent, :].astype(jnp.float32), image)
                first = jnp.where(borrowed, first - shared + half, first)
                limit = jnp.where(borrowed, sibling_rows, limit)
            for j in order[1:]:
                remote(
                    rs_in.at[k, j, part], rs_in.at[k, j, part],
                    rs_s.at[k, 0, q], rs_r.at[k, j, q], sibling, member,
                ).wait_recv()
                image = image + rs_in[k, j, part].astype(jnp.float32)
            positions = lax.broadcasted_iota(jnp.int32, (piece, width), 0) + first
            image = jnp.where(positions < limit, image, 0.0) * gain
            if not opening:
                image = image + keep * app_chunk[part, :]
            app_chunk[part, :] = image
            xbuf[k + 1, 0, mine] = image.astype(jnp.bfloat16)
            for t in range(members - 1):
                z_copy(k + 1, t, q).start()
            copies = far_copy(k + 1, member, q), near_copy(k + 1, member, q)
            for copy in copies:
                if opening:
                    copy.start()
                else:
                    pl.when(k < ITERS - 1)(copy.start)
        sent()
        return keep, gain

    for load in loads:
        load.wait()
    keep, gain = iteration(0, None, None, opening=True)
    keep, gain = lax.fori_loop(1, ITERS, lambda k, pair: iteration(k, *pair), (keep, gain))

    state = keep * cur[...] + gain * block(ITERS - 1)
    cur[...] = state
    high = state.astype(jnp.bfloat16)
    low = (state - high.astype(jnp.float32)).astype(jnp.bfloat16)
    mixed = transposed_dot(high, low)
    density[...] = transposed_dot(high, high) + (mixed + mixed.T)
    gather(ITERS, final=True)
    for q in range(tiles):
        sibling_tile(ITERS, q)
    applied = block(ITERS)
    send_sums(ITERS, state * state, state * applied, applied * applied)
    final_step = applied.astype(jnp.bfloat16)
    crossed = transposed_dot(high, final_step) + transposed_dot(low, final_step)
    crossed = crossed + crossed.T
    squared = transposed_dot(final_step, final_step)
    scal_wait(ITERS)
    keep, gain = coefficients(ITERS)
    density[...] = keep * keep * density[...] + keep * gain * crossed + gain * gain * squared
    cur[...] = keep * cur[...] + gain * applied
    slab_rows = capacity // members
    slab[...] = cur[pl.ds(pl.multiple_of(member * slab_rows, slab_rows), slab_rows), :]
    sent()
    for q in range(tiles):
        for t in range(members - 1):
            z_copy(ITERS, t, q).wait_send()


def iterate(half, guess, left_env, right_env, block_rows, charges):
    capacity, width = guess.shape
    terms = left_env.shape[0]
    sectors = lax.axis_size("sec")
    members = lax.axis_size("mpo")
    tiles = -(-half // width)
    depths = capacity // width
    lent = max(capacity - half, 16)
    entries = MEAN * sectors * width
    dma = pltpu.SemaphoreType.DMA
    vmem = pl.BlockSpec(memory_space=pltpu.VMEM)
    smem = pl.BlockSpec(memory_space=pltpu.SMEM)
    hbm = pl.BlockSpec(memory_space=pl.ANY)
    return pl.pallas_call(
        functools.partial(iterate_kernel, sectors, members, entries, half),
        out_shape=(
            jax.ShapeDtypeStruct((capacity // members, width), jnp.float32),
            jax.ShapeDtypeStruct((width, width), jnp.float32),
        ),
        in_specs=[smem, smem, vmem, hbm, hbm],
        out_specs=(vmem, vmem),
        scratch_shapes=[
            pltpu.VMEM((terms, depths, capacity, width), left_env.dtype),
            pltpu.VMEM((terms, width, width), right_env.dtype),
            pltpu.VMEM((ITERS + 1, 6, half, width), jnp.bfloat16),
            pltpu.VMEM((capacity, width), jnp.float32),
            pltpu.VMEM((half // members, width), jnp.float32),
            pltpu.VMEM((capacity, width), jnp.float32),
            pltpu.VMEM((ITERS + 1, lent, width), jnp.bfloat16),
            pltpu.VMEM((ITERS + 1, lent, width), jnp.bfloat16),
            pltpu.VMEM((ITERS, half, width), jnp.bfloat16),
            pltpu.VMEM((ITERS, members, half // members, width), jnp.bfloat16),
            pltpu.VMEM((ITERS + 1, sectors, 8, 128), jnp.float32),
            dma((depths + 1,)),
            dma((ITERS + 1, members - 1, tiles)),
            dma((ITERS + 1, members, tiles)),
            dma((ITERS + 1, members, tiles)),
            dma((ITERS + 1, members, tiles)),
            dma((ITERS + 1, members, tiles)),
            dma((ITERS + 1, members, tiles)),
            dma((ITERS + 1, tiles)),
            dma((ITERS + 1, tiles)),
            dma((ITERS, 2, tiles)),
            dma((ITERS, 2, tiles)),
            dma((ITERS + 1,)),
            dma((ITERS + 1,)),
            dma((ITERS, members - 1, tiles)),
            dma((ITERS, members, tiles)),
            dma((ITERS + 1, sectors)),
            dma((ITERS + 1, sectors)),
        ],
        compiler_params=pltpu.CompilerParams(
            collective_id=(capacity - half) // (width // 2),
            has_side_effects=True, vmem_limit_bytes=56 * 1024 * 1024,
        ),
    )(block_rows, charges, guess, left_env, right_env)


small_residual = 3e-4


def exact_dot(left, right, dims):
    return lax.dot_general(
        left, right, (dims, ((), ())), precision=highest, preferred_element_type=jnp.float32
    )


def truncate_kernel(ranks, density, slab, copied, out, gram, pair):
    width = density.shape[0]
    copied[...] = slab[...]
    rows = lax.broadcasted_iota(jnp.int32, (width, width), 0)
    lanes = lax.broadcasted_iota(jnp.int32, (width, width), 1)
    identity = jnp.where(rows == lanes, 1.0, 0.0)
    full = identity + density[...] / MEAN
    kept = ranks[lax.axis_index("sec")]
    basis = jnp.where(lanes < kept, full, 0.0)
    basis_t = jnp.where(rows < kept, full, 0.0)
    matrix = exact_dot(basis_t, basis, ((1,), (0,))) + jnp.where(rows < kept, 0.0, identity)
    gram[...] = matrix
    largest = jnp.max(jnp.sum(jnp.abs(matrix), axis=0, keepdims=True))
    scale = 2.0 / (1.0 + largest)
    pair[:width, :] = identity - scale * matrix
    pair[width:, :] = scale * identity

    def unfinished(bound):
        return bound > small_residual

    def step(bound):
        square = bound * bound
        grow = 2.0 / (2.0 - square)
        product = exact_dot(pair[...], pair[:width, :], ((1,), (0,)))
        pair[width:, :] = grow * (pair[width:, :] + product[width:, :])
        pair[:width, :] = (1.0 - grow) * identity + grow * product[:width, :]
        return square / (2.0 - square)

    lax.while_loop(unfinished, step, (largest - 1.0) / (largest + 1.0))
    inverse = pair[width:, :]
    coords = exact_dot(slab[...], basis, ((1,), (0,)))
    solved = exact_dot(coords, inverse, ((1,), (0,)))
    rest = coords - exact_dot(solved, gram[...], ((1,), (0,)))
    solved = solved + exact_dot(rest, inverse, ((1,), (0,)))
    out[...] = exact_dot(solved, basis_t, ((1,), (0,)))


def truncate(density, slab, ranks):
    width = density.shape[0]
    vmem = pl.BlockSpec(memory_space=pltpu.VMEM)
    return pl.pallas_call(
        truncate_kernel,
        out_shape=(jax.ShapeDtypeStruct(slab.shape, jnp.float32),) * 2,
        in_specs=[pl.BlockSpec(memory_space=pltpu.SMEM), vmem, vmem],
        out_specs=(vmem, vmem),
        scratch_shapes=[
            pltpu.VMEM((width, width), jnp.float32),
            pltpu.VMEM((2 * width, width), jnp.float32),
        ],
    )(ranks, density, slab)


def shards(guess, left_env, right_env, block_rows, charges, ranks):
    capacity, width = guess.shape
    ids = jnp.arange(block_rows.shape[0])
    pairs = (ids[:, None] // 2 == ids[None, :] // 2) & (ids[:, None] != ids[None, :])
    most, least = block_rows[:, None], block_rows[None, :]
    halves = [capacity - width, capacity - width // 2, capacity]
    needs = sum(
        ((most > half) & (least > 2 * half - capacity) & pairs).astype(jnp.int32) for half in halves[:-1]
    )
    choice = jnp.max(needs)
    slab, density = lax.switch(
        choice, [functools.partial(iterate, half) for half in halves],
        guess, left_env, right_env, block_rows, charges,
    )
    return truncate(density, slab, ranks)


def solution(mesh):
    return jax.shard_map(
        shards,
        mesh=mesh,
        in_specs=(P("sec", None), P("mpo", "sec", None), P("mpo", "sec", None), P(), P("mpo"), P()),
        out_specs=(P(("sec", "mpo"), None), P(("sec", "mpo"), None)),
        check_vma=False,
    )
```

```python
import functools

import jax
import jax.numpy as jnp
from jax import lax
from jax.experimental import pallas as pl
from jax.experimental.pallas import tpu as pltpu
from jax.sharding import PartitionSpec as P

MEAN = 256
ITERS = 4


epsilon = 1e-06
step_size = 0.1
highest = lax.Precision.HIGHEST


def row_sum(values):
    return jnp.sum(jnp.sum(values.reshape(-1, 8, 128), axis=0), axis=0, keepdims=True)


def arrival_order(member, members):
    steps = [(-1, 1), (1, -1)][member >= members // 2]
    order = [member]
    for d in range(1, members):
        order += [member + s * d for s in steps if 0 <= member + s * d < members]
    return order


def transposed_dot(left, right):
    return lax.dot_general(left, right, (((0,), (0,)), ((), ())), preferred_element_type=jnp.float32)


def iterate_kernel(
    sectors, members, entries, half,
    block_rows, charges, guess, left_hbm, right_hbm, slab, density,
    left, right, xbuf, acc, app_chunk, cur, ex_out, ex_in, rs_out, rs_in, scal,
    load_sem, z_s, z_r, n_s, n_r, f_s, f_r, b_s, b_r, p_s, p_r, e_s, e_r, rs_s, rs_r, sc_s, sc_r,
):
    sector = lax.axis_index("sec")
    member = lax.axis_index("mpo")
    capacity, width = guess.shape
    packed = half < capacity
    shared = 2 * half - capacity
    tiles = -(-half // width)
    depths = left.shape[1]

    def deep(q):
        return min(width, half - q * width)

    def piece_rows(q):
        return deep(q) // members

    def part_of(q):
        return pl.ds(q * width // members, piece_rows(q))

    terms = left.shape[0]
    chips = sectors // 2
    parity = lax.rem(sector, 2)
    chip = sector // 2
    odd = lax.rem(chip, 2)
    sibling = sector + 1 - 2 * parity
    ahead = lax.rem(sector + 2, sectors)
    behind = lax.rem(sector + sectors - 2, sectors)
    square = chips == 4
    sends = []

    loads = [pltpu.make_async_copy(right_hbm, right, load_sem.at[depths])]
    for i in range(depths):
        loads.append(pltpu.make_async_copy(
            left_hbm.at[:, :, pl.ds(i * width, width)], left.at[:, i], load_sem.at[i]
        ))
    for load in loads:
        load.start()

    barrier = pltpu.get_barrier_semaphore()
    for d in range(1, sectors):
        pl.semaphore_signal(
            barrier, inc=1, device_id=(lax.rem(sector + d, sectors), member),
            device_id_type=pl.DeviceIdType.MESH,
        )
    for d in range(1, members):
        pl.semaphore_signal(
            barrier, inc=1, device_id=(sector, lax.rem(member + d, members)),
            device_id_type=pl.DeviceIdType.MESH,
        )
    pl.semaphore_wait(barrier, sectors + members - 2)

    def remote(src, dst, send, recv, sec, mpo):
        return pltpu.make_async_remote_copy(
            src_ref=src, dst_ref=dst, send_sem=send, recv_sem=recv,
            device_id=(sec, mpo), device_id_type=pl.DeviceIdType.MESH,
        )

    def launch(copy):
        copy.start()
        sends.append(copy)

    def sent():
        while sends:
            sends.pop().wait_send()

    def by_member(table):
        value = jnp.int32(table[0])
        for m in range(1, members):
            value = jnp.where(member == m, table[m], value)
        return value

    def tile_rows(q):
        return pl.ds(q * width, deep(q))

    def piece_of(j, q):
        return pl.ds(pl.multiple_of(q * width + j * piece_rows(q), piece_rows(q)), piece_rows(q))

    order = [by_member([arrival_order(m, members)[r] for m in range(members)]) for r in range(members)]
    targets = order[1:]
    if square:
        near = jnp.where(odd == 1, behind, ahead)
        across = lax.rem(sector + sectors // 2, sectors)
        distant = jnp.where(odd == 1, ahead, behind)
        near_shift = jnp.where(odd == 1, 2, -2)
        fifth_far = parity == odd
    else:
        near, distant = behind, ahead
        near_shift = jnp.int32(-2)
        fifth_far = parity == 0
    far_shift = -near_shift

    def z_copy(k, t, q):
        rows = piece_of(member, q)
        return remote(
            xbuf.at[k, 0, rows], xbuf.at[k, 0, rows], z_s.at[k, t, q], z_r.at[k, member, q],
            sector, targets[t],
        )

    def z_wait(k, j, q):
        arrived(k, 0, piece_of(j, q), z_s.at[k, 0, q], z_r.at[k, j, q])

    def near_copy(k, j, q):
        rows = piece_of(j, q)
        return remote(
            xbuf.at[k, 0, rows], xbuf.at[k, 2, rows], n_s.at[k, j, q], n_r.at[k, j, q], near, member,
        )

    def far_copy(k, j, q):
        rows = piece_of(j, q)
        return remote(
            xbuf.at[k, 0, rows], xbuf.at[k, 3, rows], f_s.at[k, j, q], f_r.at[k, j, q], distant, member,
        )

    def far_relay(k, j, q):
        rows = piece_of(j, q)
        launch(remote(
            xbuf.at[k, 2, rows], xbuf.at[k, 3, rows], f_s.at[k, j, q], f_r.at[k, j, q], across, member,
        ))

    def sibling_send(k, q):
        rows = tile_rows(q)
        launch(remote(
            xbuf.at[k, 0, rows], xbuf.at[k, 1, rows], b_s.at[k, q], b_r.at[k, q], sibling, member,
        ))

    def pass_send(k, q, far):
        rows = tile_rows(q)
        launch(remote(
            xbuf.at[k, 2 + far, rows], xbuf.at[k, 4 + far, rows],
            p_s.at[k, far, q], p_r.at[k, far, q], sibling, member,
        ))

    def exchange(k):
        return remote(ex_out.at[k], ex_in.at[k], e_s.at[k], e_r.at[k], sibling, member)

    def arrived(k, slot, rows, send, recv):
        remote(xbuf.at[k, slot, rows], xbuf.at[k, slot, rows], send, recv, sibling, member).wait_recv()

    def rs_copy(k, t, q):
        return remote(
            rs_out.at[k, piece_of(targets[t], q)], rs_in.at[k, member, part_of(q)],
            rs_s.at[k, t, q], rs_r.at[k, member, q], sector, targets[t],
        )

    def scal_copy(k, d):
        return remote(
            scal.at[k, sector], scal.at[k, sector],
            sc_s.at[k, d - 1], sc_r.at[k, d - 1], lax.rem(sector + d, sectors), member,
        )

    def scal_wait(k):
        for d in range(1, sectors):
            src = lax.rem(sector - d + sectors, sectors)
            remote(
                scal.at[k, src], scal.at[k, src],
                sc_s.at[k, d - 1], sc_r.at[k, d - 1], src, member,
            ).wait_recv()

    def term_of(charge):
        index = jnp.int32(0)
        for i in range(1, terms):
            index = jnp.where(charges[i] == charge, i, index)
        return index

    def count_of(shift):
        return block_rows[lax.rem(sector + shift + sectors, sectors)]

    own_rows, sibling_rows = count_of(0), block_rows[sibling]
    fifth = 2 * parity - 1
    both_far = jnp.where(fifth_far, 1, 0)
    term_own, term_sibling = term_of(0), term_of(2 * parity - 1)
    term_near, term_far, term_fifth = term_of(near_shift), term_of(far_shift), term_of(-fifth)

    def over(rows):
        return jnp.where(rows > half, 1, 0)

    mates = 1 - 2 * parity
    fifth_slot = 4 + both_far
    far_rows, near_rows = count_of(-far_shift), count_of(-near_shift)
    near_tail = over(count_of(-near_shift + mates))
    far_tail = over(count_of(-far_shift + mates))
    tasks = {
        0: (0, term_own, term_sibling, over(sibling_rows), 1),
        1: (1, term_sibling, term_own, over(own_rows), 1),
        2: (2, term_near, term_fifth, near_tail, 1 - both_far),
        3: (3, term_far, term_fifth, far_tail, both_far),
        4: (fifth_slot, term_fifth, term_fifth, 0, 1),
    }
    ends = (
        (term_near, over(near_rows), 1 - both_far), (term_far, over(far_rows), both_far),
    )

    def mix(k, slot, q, index, keep_rows=None):
        value = xbuf[k, slot, tile_rows(q), :]
        if keep_rows is not None:
            value = jnp.where(keep_rows > 0, value, jnp.zeros_like(value))
        return jnp.dot(value, right[index], preferred_element_type=jnp.float32).astype(jnp.bfloat16)

    def tile_task(k, group, q):
        slot, index, mate, tail, counted = tasks[group]
        keep_rows = None
        if not packed or q * width < shared or group == 4:
            tail = None
        else:
            index = jnp.where(tail > 0, mate, index)
            keep_rows = 1 - tail * (1 - counted)
        return index, q, tail, mix(k, slot, q, index, keep_rows)

    def passed_task(k, q, far):
        index, tail, counted = ends[far]
        index = jnp.where(tail > 0, index, term_fifth)
        return index, q, tail, mix(k, 4 + far, q, index, jnp.maximum(tail, counted))

    def add(task, rows=pl.ds(0, capacity), first=False):
        index, q, tail, mixed = task
        column = half + q * width - shared
        if tail is None:
            factor = left[index, q, rows, pl.ds(0, deep(q))]
        elif column % width == 0:
            factor = left[index, jnp.where(tail > 0, column // width, q), rows, pl.ds(0, deep(q))]
        else:
            factor = jnp.where(
                tail > 0, left[index, column // width, rows, pl.ds(column % width, deep(q))],
                left[index, q, rows, pl.ds(0, deep(q))],
            )
        value = jnp.dot(factor, mixed, preferred_element_type=jnp.float32)
        acc[rows, :] = value if first else acc[rows, :] + value

    def block(k):
        if not packed:
            return xbuf[k, 0].astype(jnp.float32)
        ending = xbuf[k, 0, pl.ds(shared, half - shared), :]
        beyond = xbuf[k, 1, pl.ds(shared, half - shared), :]
        return jnp.concatenate([
            xbuf[k, 0, pl.ds(0, shared), :],
            jnp.where(sibling_rows > half, jnp.zeros_like(ending), ending),
            jnp.where(own_rows > half, beyond, jnp.zeros_like(beyond)),
        ], axis=0).astype(jnp.float32)

    def send_sums(k, first, second, third):
        rows = [row_sum(first), row_sum(second), row_sum(third), jnp.zeros((5, 128), jnp.float32)]
        scal[k, sector] = jnp.concatenate(rows, axis=0)
        for d in range(1, sectors):
            launch(scal_copy(k, d))

    def coefficients(k, opening=False):
        sums = jnp.sum(jnp.sum(scal[k], axis=0), axis=1, keepdims=True)
        self_dot, cross_dot, image_dot = sums[0:1], sums[1:2], sums[2:3]
        if opening:
            scale = lax.rsqrt(self_dot / entries + epsilon)
            return scale, scale
        rayleigh = cross_dot / (self_dot + epsilon)
        squares = self_dot * (1.0 - (step_size * rayleigh) ** 2) + step_size**2 * image_dot
        scale = lax.rsqrt(squares / entries + epsilon)
        return (1.0 + step_size * rayleigh) * scale, -step_size * scale

    def state_sums(k, keep, gain):
        state = keep * cur[...] + jnp.where(k == 1, 0.0, gain) * block(k - 1)
        cur[...] = state
        applied = block(k)
        send_sums(k, state * state, state * applied, applied * applied)

    def pack(k, q, rows):
        if not packed or q * width < shared:
            return rows
        if q * width == shared:
            exchange(k).wait_recv()
        return jnp.where(sibling_rows > half, ex_in[k, pl.ds(q * width - shared, deep(q)), :], rows)

    def offer(k, rows):
        ex_out[k] = rows.astype(jnp.bfloat16)
        launch(exchange(k))

    positions = lax.broadcasted_iota(jnp.int32, (capacity, width), 0)
    start = jnp.where(positions < own_rows, guess[...], 0.0)
    cur[...] = start
    if packed:
        offer(ITERS, cur[pl.ds(half, capacity - half), :])
    for q in range(tiles):
        xbuf[0, 0, tile_rows(q)] = pack(ITERS, q, cur[tile_rows(q), :].astype(jnp.bfloat16))
        for j in range(members):
            launch(near_copy(0, j, q))
            if not square:
                launch(far_copy(0, j, q))
        sibling_send(0, q)

    def near_tile(k, q, opening=False):
        for j in order:
            arrived(k, 2, piece_of(j, q), n_s.at[k, j, q], n_r.at[k, j, q])
            if opening and square:
                far_relay(k, j, q)
        pass_send(k, q, 0)

    def far_tile(k, q):
        for j in order:
            arrived(k, 3, piece_of(j, q), f_s.at[k, j, q], f_r.at[k, j, q])
        pass_send(k, q, 1)

    def sibling_tile(k, q):
        arrived(k, 1, tile_rows(q), b_s.at[k, q], b_r.at[k, q])

    def passed_tile(k, q, far):
        arrived(k, 4 + far, tile_rows(q), p_s.at[k, far, q], p_r.at[k, far, q])

    def gather(k, final=False):
        for q in range(tiles):
            for j in order[1:]:
                z_wait(k, j, q)
                if not final:
                    launch(far_copy(k, j, q))
                    launch(near_copy(k, j, q))
            sibling_send(k, q)
            if not final:
                add(tile_task(k, 0, q), first=q == 0)

    def iteration(k, keep, gain, opening=False):
        if opening:
            for q in range(tiles):
                add(tile_task(k, 0, q), first=q == 0)
        else:
            gather(k)
        for q in range(tiles):
            if not opening:
                near_tile(k, q)
            elif q == 0:
                for p in range(tiles):
                    near_tile(k, p, opening)
            add(tile_task(k, 2, q))
            far_tile(k, q)
            if q == tiles - 1:
                passed_tile(k, q, 0)
                if packed:
                    add(passed_task(k, q, 0))
            add(tile_task(k, 3, q))
            if q == 0:
                for i in range(tiles):
                    sibling_tile(k, i)
                    add(tile_task(k, 1, i))
            if q < tiles - 1:
                passed_tile(k, q, 0)
                passed_tile(k, q, 1)
                if packed and q * width >= shared:
                    add(passed_task(k, q, 0))
                    add(passed_task(k, q, 1))
                else:
                    add(tile_task(k, 4, q))
        passed_tile(k, tiles - 1, 1)
        if packed:
            last = passed_task(k, tiles - 1, 1)
            rows = pl.ds(half, capacity - half)
            add(last, rows)
            offer(k, acc[rows, :])
        else:
            last = tile_task(k, 4, tiles - 1)
        earlier = list(sends)
        sends.clear()
        for q in range(tiles):
            add(last, tile_rows(q))
            rs_out[k, tile_rows(q)] = pack(k, q, acc[tile_rows(q), :].astype(jnp.bfloat16))
            for t in range(members - 1):
                launch(rs_copy(k, t, q))
        if opening:
            nothing = jnp.zeros((8, 128))
            send_sums(0, cur[...] * cur[...], nothing, nothing)
        else:
            state_sums(k, keep, gain)
        for copy in earlier:
            copy.wait_send()
        scal_wait(k)
        keep, gain = coefficients(k, opening)
        if not opening:
            for q in range(tiles):
                for t in range(members - 1):
                    z_copy(k, t, q).wait_send()
                far_copy(k, member, q).wait_send()
                near_copy(k, member, q).wait_send()
        for q in range(tiles):
            part, piece = part_of(q), piece_rows(q)
            mine = piece_of(member, q)
            image = acc[mine, :]
            first, limit = member * piece + q * width, own_rows
            if packed and q * width >= shared:
                borrowed = sibling_rows > half
                lent = pl.ds(pl.multiple_of(q * width - shared + member * piece, piece), piece)
                image = jnp.where(borrowed, ex_in[k, lent, :].astype(jnp.float32), image)
                first = jnp.where(borrowed, first - shared + half, first)
                limit = jnp.where(borrowed, sibling_rows, limit)
            for j in order[1:]:
                remote(
                    rs_in.at[k, j, part], rs_in.at[k, j, part],
                    rs_s.at[k, 0, q], rs_r.at[k, j, q], sibling, member,
                ).wait_recv()
                image = image + rs_in[k, j, part].astype(jnp.float32)
            positions = lax.broadcasted_iota(jnp.int32, (piece, width), 0) + first
            image = jnp.where(positions < limit, image, 0.0) * gain
            if not opening:
                image = image + keep * app_chunk[part, :]
            app_chunk[part, :] = image
            xbuf[k + 1, 0, mine] = image.astype(jnp.bfloat16)
            for t in range(members - 1):
                z_copy(k + 1, t, q).start()
            copies = far_copy(k + 1, member, q), near_copy(k + 1, member, q)
            for copy in copies:
                if opening:
                    copy.start()
                else:
                    pl.when(k < ITERS - 1)(copy.start)
        sent()
        return keep, gain

    for load in loads:
        load.wait()
    keep, gain = iteration(0, None, None, opening=True)
    keep, gain = lax.fori_loop(1, ITERS, lambda k, pair: iteration(k, *pair), (keep, gain))

    state = keep * cur[...] + gain * block(ITERS - 1)
    cur[...] = state
    high = state.astype(jnp.bfloat16)
    low = (state - high.astype(jnp.float32)).astype(jnp.bfloat16)
    mixed = transposed_dot(high, low)
    density[...] = transposed_dot(high, high) + (mixed + mixed.T)
    gather(ITERS, final=True)
    for q in range(tiles):
        sibling_tile(ITERS, q)
    applied = block(ITERS)
    send_sums(ITERS, state * state, state * applied, applied * applied)
    final_step = applied.astype(jnp.bfloat16)
    crossed = transposed_dot(high, final_step) + transposed_dot(low, final_step)
    crossed = crossed + crossed.T
    squared = transposed_dot(final_step, final_step)
    scal_wait(ITERS)
    keep, gain = coefficients(ITERS)
    density[...] = keep * keep * density[...] + keep * gain * crossed + gain * gain * squared
    cur[...] = keep * cur[...] + gain * applied
    slab_rows = capacity // members
    slab[...] = cur[pl.ds(pl.multiple_of(member * slab_rows, slab_rows), slab_rows), :]
    sent()
    for q in range(tiles):
        for t in range(members - 1):
            z_copy(ITERS, t, q).wait_send()


def iterate(half, guess, left_env, right_env, block_rows, charges):
    capacity, width = guess.shape
    terms = left_env.shape[0]
    sectors = lax.axis_size("sec")
    members = lax.axis_size("mpo")
    tiles = -(-half // width)
    depths = capacity // width
    lent = max(capacity - half, 16)
    entries = MEAN * sectors * width
    dma = pltpu.SemaphoreType.DMA
    vmem = pl.BlockSpec(memory_space=pltpu.VMEM)
    smem = pl.BlockSpec(memory_space=pltpu.SMEM)
    hbm = pl.BlockSpec(memory_space=pl.ANY)
    return pl.pallas_call(
        functools.partial(iterate_kernel, sectors, members, entries, half),
        out_shape=(
            jax.ShapeDtypeStruct((capacity // members, width), jnp.float32),
            jax.ShapeDtypeStruct((width, width), jnp.float32),
        ),
        in_specs=[smem, smem, vmem, hbm, hbm],
        out_specs=(vmem, vmem),
        scratch_shapes=[
            pltpu.VMEM((terms, depths, capacity, width), left_env.dtype),
            pltpu.VMEM((terms, width, width), right_env.dtype),
            pltpu.VMEM((ITERS + 1, 6, half, width), jnp.bfloat16),
            pltpu.VMEM((capacity, width), jnp.float32),
            pltpu.VMEM((half // members, width), jnp.float32),
            pltpu.VMEM((capacity, width), jnp.float32),
            pltpu.VMEM((ITERS + 1, lent, width), jnp.bfloat16),
            pltpu.VMEM((ITERS + 1, lent, width), jnp.bfloat16),
            pltpu.VMEM((ITERS, half, width), jnp.bfloat16),
            pltpu.VMEM((ITERS, members, half // members, width), jnp.bfloat16),
            pltpu.VMEM((ITERS + 1, sectors, 8, 128), jnp.float32),
            dma((depths + 1,)),
            dma((ITERS + 1, members - 1, tiles)),
            dma((ITERS + 1, members, tiles)),
            dma((ITERS + 1, members, tiles)),
            dma((ITERS + 1, members, tiles)),
            dma((ITERS + 1, members, tiles)),
            dma((ITERS + 1, members, tiles)),
            dma((ITERS + 1, tiles)),
            dma((ITERS + 1, tiles)),
            dma((ITERS, 2, tiles)),
            dma((ITERS, 2, tiles)),
            dma((ITERS + 1,)),
            dma((ITERS + 1,)),
            dma((ITERS, members - 1, tiles)),
            dma((ITERS, members, tiles)),
            dma((ITERS + 1, sectors)),
            dma((ITERS + 1, sectors)),
        ],
        compiler_params=pltpu.CompilerParams(
            collective_id=(capacity - half) // (width // 2),
            has_side_effects=True, vmem_limit_bytes=56 * 1024 * 1024,
        ),
    )(block_rows, charges, guess, left_env, right_env)


small_residual = 3e-4


def exact_dot(left, right, dims):
    return lax.dot_general(
        left, right, (dims, ((), ())), precision=highest, preferred_element_type=jnp.float32
    )


def truncate_kernel(ranks, density, slab, copied, out, gram, pair):
    width = density.shape[0]
    copied[...] = slab[...]
    rows = lax.broadcasted_iota(jnp.int32, (width, width), 0)
    lanes = lax.broadcasted_iota(jnp.int32, (width, width), 1)
    identity = jnp.where(rows == lanes, 1.0, 0.0)
    full = identity + density[...] / MEAN
    kept = ranks[lax.axis_index("sec")]
    basis = jnp.where(lanes < kept, full, 0.0)
    basis_t = jnp.where(rows < kept, full, 0.0)
    matrix = exact_dot(basis_t, basis, ((1,), (0,))) + jnp.where(rows < kept, 0.0, identity)
    gram[...] = matrix
    largest = jnp.max(jnp.sum(jnp.abs(matrix), axis=0, keepdims=True))
    scale = 2.0 / (1.0 + largest)
    pair[:width, :] = identity - scale * matrix
    pair[width:, :] = scale * identity

    def unfinished(bound):
        return bound > small_residual

    def step(bound):
        square = bound * bound
        grow = 2.0 / (2.0 - square)
        product = exact_dot(pair[...], pair[:width, :], ((1,), (0,)))
        pair[width:, :] = grow * (pair[width:, :] + product[width:, :])
        pair[:width, :] = (1.0 - grow) * identity + grow * product[:width, :]
        return square / (2.0 - square)

    lax.while_loop(unfinished, step, (largest - 1.0) / (largest + 1.0))
    inverse = pair[width:, :]
    coords = exact_dot(slab[...], basis, ((1,), (0,)))
    solved = exact_dot(coords, inverse, ((1,), (0,)))
    rest = coords - exact_dot(solved, gram[...], ((1,), (0,)))
    solved = solved + exact_dot(rest, inverse, ((1,), (0,)))
    out[...] = exact_dot(solved, basis_t, ((1,), (0,)))


def truncate(density, slab, ranks):
    width = density.shape[0]
    vmem = pl.BlockSpec(memory_space=pltpu.VMEM)
    return pl.pallas_call(
        truncate_kernel,
        out_shape=(jax.ShapeDtypeStruct(slab.shape, jnp.float32),) * 2,
        in_specs=[pl.BlockSpec(memory_space=pltpu.SMEM), vmem, vmem],
        out_specs=(vmem, vmem),
        scratch_shapes=[
            pltpu.VMEM((width, width), jnp.float32),
            pltpu.VMEM((2 * width, width), jnp.float32),
        ],
    )(ranks, density, slab)


def shards(guess, left_env, right_env, block_rows, charges, ranks):
    capacity, width = guess.shape
    pairs = block_rows.reshape(-1, 2)
    most, least = jnp.max(pairs, axis=1), jnp.min(pairs, axis=1)
    halves = [capacity - width, capacity - width // 2, capacity]
    needs = sum(
        ((most > half) & (least > 2 * half - capacity)).astype(jnp.int32) for half in halves[:-1]
    )
    choice = jnp.max(needs)
    slab, density = lax.switch(
        choice, [functools.partial(iterate, half) for half in halves],
        guess, left_env, right_env, block_rows, charges,
    )
    return truncate(density, slab, ranks)


def solution(mesh):
    return jax.shard_map(
        shards,
        mesh=mesh,
        in_specs=(P("sec", None), P("mpo", "sec", None), P("mpo", "sec", None), P(), P("mpo"), P()),
        out_specs=(P(("sec", "mpo"), None), P(("sec", "mpo"), None)),
        check_vma=False,
    )
```
